32 devices in a mesh: ctx: 8 (over z, core), tab: 4 (over y, x).
Axes of the slice: x: 2, y: 2, z: 4, core: 2. Of those that a mesh axis runs over, the one named last changes fastest.
Arguments:
- queries: bfloat16 [32, 4, 8192], P(('ctx', 'tab')), may hold values from -80 to 80
- prefix_key_value: bfloat16 [4096, 2, 1024], P('ctx'), may hold values from -6 to 6
- tab_key_value: bfloat16 [4, 512, 2, 1024], P('tab', 'ctx'), may hold values from -6 to 6
- tab_owner: int32 [4], replicated, may hold values from 0 to 3, each once
- session_tab: int32 [32], P(('ctx', 'tab')), may hold values from 0 to 3
- suffix_key_value: bfloat16 [32, 256, 2, 1024], P(('ctx', 'tab')), may hold values from -6 to 6
- suffix_len: int32 [32], P(('ctx', 'tab')), may hold values from 1 to 256, as said below
- token_keys: bfloat16 [32, 4, 1024], P(('ctx', 'tab')), may hold values from -12 to 12
- token_values: bfloat16 [32, 4, 1024], P(('ctx', 'tab')), may hold values from -6 to 6
Outputs:
- attention: bfloat16 [32, 4, 8192], P(('ctx', 'tab'))
The draws below stay inside these ranges and needn't reach their ends.
Inputs may be any that keep to these rules, and one draw needn't show every extreme that they name: `tab_owner`: each tab has its own slot. `suffix_len`: some session of every draw uses all 256 slots.
All inputs are finite; a program needn't handle non-finite values.
Results may differ from the reference program's by a relative error of at most 0.0023.
Values may be sent and summed in bfloat16 or wider, within the bound.
No kernel may reach another device: no remote copies, remote signals or barrier semaphores. Data moves between devices by JAX's collectives and lax.ppermute only.
A program may use at most 64 MiB of HBM per device.

```python
import math
import jax
import jax.numpy as jnp
import numpy as np
from jax import lax

QUERY_HEADS = 64
KEY_VALUE_HEADS = 8
HEAD_SIZE = 128
DECODE_STEPS = 4
PREFIX_PER_INDEX = 512
TAB_PER_INDEX = 64
SUFFIX_SLOTS = 256
SESSION_COUNT = 32
PREFIX_TOKENS = 4096
TAB_TOKENS = 512
TAB_COUNT = 4
N_CTX = 8


def draw_queries(key, part):
    shape_all = (SESSION_COUNT, DECODE_STEPS, QUERY_HEADS * HEAD_SIZE)
    values = jnp.clip(2.0 * jax.random.normal(key, shape_all, jnp.float32), -16.0, 16.0)
    return values.astype(jnp.bfloat16)


def draw_suffix_len(key, part):
    first_key, second_key = jax.random.split(key)
    lengths = jax.random.randint(first_key, (SESSION_COUNT,), 1, SUFFIX_SLOTS + 1, jnp.int32)
    full_index = jax.random.randint(second_key, (), 0, SESSION_COUNT, jnp.int32)
    return jnp.where(jnp.arange(SESSION_COUNT, dtype=jnp.int32) == full_index, SUFFIX_SLOTS, lengths).astype(jnp.int32)


def set_ends(values, stream_key, smallest, top_value):
    extent = values.shape
    place = [jax.random.randint(jax.random.fold_in(stream_key, axis), (), 0, extent[axis]) for axis in range(len(extent))]
    values = values.at[tuple(place)].set(smallest)
    longest = extent.index(max(extent))
    place[longest] = (place[longest] + 1) % extent[longest]
    return values.at[tuple(place)].set(top_value)


def steps_of(key, dims, cuts, low, high):
    factor_of = 1.0
    for axis_at, blocks in cuts:
        steps = jax.random.uniform(jax.random.fold_in(jax.random.fold_in(key, 6), axis_at), (blocks,), jnp.float32, low / len(cuts), high / len(cuts))
        factor_of = factor_of * jnp.repeat(jnp.exp(steps), dims[axis_at] // blocks).reshape((-1,) + (1,) * (len(dims) - 1 - axis_at))
    return factor_of


def rank_table(number_of, slope):
    portions = [(1 << 20) // math.isqrt(rank ** slope) + 1 for rank in range(1, number_of + 1)]
    spread = 1 + sum(portions) // (1 << 30)
    return np.cumsum(np.array([max(1, weight // spread) for weight in portions]))


def ranked_ids(own_key, shape, amount, skew):
    grid = rank_table(amount, skew)
    ticket = jax.random.randint(jax.random.fold_in(own_key, 1), shape, 0, int(grid[amount - 1]))
    grade = jnp.searchsorted(jnp.asarray(grid, jnp.int32), ticket, side="right")
    return jax.random.permutation(jax.random.fold_in(own_key, 2), amount)[grade].astype(jnp.int32)


def bell_draw(rng, extent, deviation, most, cuts=(), held_as=jnp.bfloat16):
    values = jax.random.normal(rng, extent, jnp.float32) * deviation
    if len(cuts) > 0:
        values = steps_of(rng, extent, cuts, -0.22, 0.18) * values
    return jnp.clip(values, min=-most, max=most).astype(held_as)


def setup_inputs(seed: int = 0) -> dict:
    splits = jax.random.split(jax.random.key(seed), 10)
    return {
        "queries": draw_queries(jax.random.fold_in(splits[9], 71), 0),
        "prefix_key_value": bell_draw(splits[1], (PREFIX_TOKENS, 2, KEY_VALUE_HEADS * HEAD_SIZE), 1.0, 6.0, ((0, 8),)),
        "tab_key_value": bell_draw(splits[2], (TAB_COUNT, TAB_TOKENS, 2, KEY_VALUE_HEADS * HEAD_SIZE), 1.0, 6.0, ((0, 4), (1, 8))),
        "tab_owner": jax.random.permutation(splits[3], TAB_COUNT).astype(jnp.int32),
        "session_tab": set_ends(ranked_ids(splits[4], (SESSION_COUNT,), TAB_COUNT, 2), jax.random.fold_in(splits[4], 3), 0, TAB_COUNT - 1).astype(jnp.int32),
        "suffix_key_value": bell_draw(splits[5], (SESSION_COUNT, SUFFIX_SLOTS, 2, KEY_VALUE_HEADS * HEAD_SIZE), 1.0, 6.0, ((0, 32),)),
        "suffix_len": draw_suffix_len(jax.random.fold_in(splits[9], 71), 0),
        "token_keys": bell_draw(splits[7], (SESSION_COUNT, DECODE_STEPS, KEY_VALUE_HEADS * HEAD_SIZE), 2.0, 12.0, ((0, 32),)),
        "token_values": bell_draw(splits[8], (SESSION_COUNT, DECODE_STEPS, KEY_VALUE_HEADS * HEAD_SIZE), 1.0, 6.0, ((0, 32),)),
    }


NEGATIVE_FILLER = -1.0e30


def rounded_weights(scores):
    largest = jnp.max(scores, axis=-1)
    weights = lax.optimization_barrier(jnp.exp(scores - largest[..., None]).astype(jnp.bfloat16)).astype(jnp.float32)
    return largest, weights, jnp.sum(weights, axis=-1)


def level_state(queries_block, keys_block, values_block, valid):
    scores = jnp.einsum("rtkgd,rnkd->rtkgn", queries_block, keys_block, precision=lax.Precision.HIGHEST) * (HEAD_SIZE ** -0.5)
    scores = jnp.where(valid[:, :, None, None, :], scores, NEGATIVE_FILLER)
    largest, weights, totals = rounded_weights(scores)
    summed = jnp.einsum("rtkgn,rnkd->rtkgd", weights, values_block, precision=lax.Precision.HIGHEST)
    return largest, totals, summed


def combine_states(earlier, later):
    largest = jnp.maximum(earlier[0], later[0])
    weight_one = jnp.exp(earlier[0] - largest)
    weight_two = jnp.exp(later[0] - largest)
    return (largest, earlier[1] * weight_one + later[1] * weight_two,
            earlier[2] * weight_one[..., None] + later[2] * weight_two[..., None])


def reference(queries, prefix_key_value, tab_key_value, tab_owner, session_tab, suffix_key_value, suffix_len, token_keys, token_values):
    group_count = QUERY_HEADS // KEY_VALUE_HEADS
    slots = tab_owner[session_tab].astype(jnp.int32)
    query_head_count = queries.astype(jnp.float32).reshape(SESSION_COUNT, DECODE_STEPS, KEY_VALUE_HEADS, group_count, HEAD_SIZE)
    shared_prefix = prefix_key_value.astype(jnp.float32).reshape(N_CTX, PREFIX_PER_INDEX, 2, KEY_VALUE_HEADS, HEAD_SIZE)
    every_tab = tab_key_value.astype(jnp.float32).reshape(TAB_COUNT, N_CTX, TAB_PER_INDEX, 2, KEY_VALUE_HEADS, HEAD_SIZE)
    cache_tensors = suffix_key_value.astype(jnp.float32).reshape(SESSION_COUNT, SUFFIX_SLOTS, 2, KEY_VALUE_HEADS, HEAD_SIZE)
    newest_keys = token_keys.astype(jnp.float32).reshape(SESSION_COUNT, DECODE_STEPS, KEY_VALUE_HEADS, HEAD_SIZE)
    newest_values = token_values.astype(jnp.float32).reshape(SESSION_COUNT, DECODE_STEPS, KEY_VALUE_HEADS, HEAD_SIZE)
    block_group = math.gcd(SESSION_COUNT, 16)
    steps_index = jnp.arange(DECODE_STEPS, dtype=jnp.int32)
    fresh_valid = steps_index[None, :] <= steps_index[:, None]

    def per_block(packed):
        queries_block, slot_block, cache_block, length_block, keys_fresh, values_fresh = packed

        def per_shard(state, shard_index):
            tab_rows = every_tab[slot_block, shard_index]
            shared_rows = jnp.broadcast_to(shared_prefix[shard_index][None], (block_group,) + shared_prefix.shape[1:])
            joined = jnp.concatenate([shared_rows, tab_rows], axis=1)
            valid = jnp.ones((block_group, DECODE_STEPS, PREFIX_PER_INDEX + TAB_PER_INDEX), dtype=bool)
            return combine_states(state, level_state(queries_block, joined[:, :, 0], joined[:, :, 1], valid)), 0

        starting_state = (jnp.full((block_group, DECODE_STEPS, KEY_VALUE_HEADS, group_count), NEGATIVE_FILLER, jnp.float32),
                   jnp.zeros((block_group, DECODE_STEPS, KEY_VALUE_HEADS, group_count), jnp.float32),
                   jnp.zeros((block_group, DECODE_STEPS, KEY_VALUE_HEADS, group_count, HEAD_SIZE), jnp.float32))
        state, ignored = lax.scan(per_shard, starting_state, jnp.arange(N_CTX, dtype=jnp.int32))
        cache_valid = jnp.arange(SUFFIX_SLOTS, dtype=jnp.int32)[None, :] < length_block[:, None]
        valid = jnp.concatenate([jnp.broadcast_to(cache_valid[:, None, :], (block_group, DECODE_STEPS, SUFFIX_SLOTS)),
                                 jnp.broadcast_to(fresh_valid[None], (block_group, DECODE_STEPS, DECODE_STEPS))], axis=-1)
        keys_joined = jnp.concatenate([cache_block[:, :, 0], keys_fresh], axis=1)
        values_joined = jnp.concatenate([cache_block[:, :, 1], values_fresh], axis=1)
        state = combine_states(state, level_state(queries_block, keys_joined, values_joined, valid))
        result = state[2] / state[1][..., None]
        return result.reshape(block_group, DECODE_STEPS, QUERY_HEADS * HEAD_SIZE).astype(jnp.bfloat16)

    count_blocks = SESSION_COUNT // block_group
    packed_all = (query_head_count.reshape((count_blocks, block_group) + query_head_count.shape[1:]),
                  slots.reshape(count_blocks, block_group),
                  cache_tensors.reshape((count_blocks, block_group) + cache_tensors.shape[1:]),
                  suffix_len.astype(jnp.int32).reshape(count_blocks, block_group),
                  newest_keys.reshape((count_blocks, block_group) + newest_keys.shape[1:]),
                  newest_values.reshape((count_blocks, block_group) + newest_values.shape[1:]))
    outputs = lax.map(per_block, packed_all)
    return outputs.reshape(SESSION_COUNT, DECODE_STEPS, QUERY_HEADS * HEAD_SIZE)
```

```python
import functools

import jax
import jax.numpy as jnp
from jax import lax
from jax.experimental import pallas as pl
from jax.experimental.pallas import tpu as pltpu
from jax.sharding import PartitionSpec as P

KEY_VALUE_HEADS = 8
HEAD_SIZE = 128
SCALE = HEAD_SIZE**-0.5
FILLER = -1e30
VMEM_LIMIT = 56 * 1024 * 1024
CODE_TOP = 32000.0
REST_TOP = 65000.0

NT = (((1,), (1,)), ((), ()))


def head_lanes(h):
    return pl.ds(h * HEAD_SIZE, HEAD_SIZE)


def put_lane(slab, lane, column):
    at = lax.broadcasted_iota(jnp.int32, slab.shape, 1)
    return jnp.where(at == lane, column, slab)


def block_softmax(score_parts, value_parts):
    largest = functools.reduce(
        jnp.maximum, [jnp.max(s, axis=-1, keepdims=True) for s in score_parts]
    )
    total, summed = 0.0, 0.0
    for scores, values in zip(score_parts, value_parts):
        weights = jnp.exp(scores - largest).astype(jnp.bfloat16)
        total += jnp.sum(weights.astype(jnp.float32), axis=-1, keepdims=True)
        summed += jnp.dot(weights, values, preferred_element_type=jnp.float32)
    return summed / total, largest + jnp.log(total)


def context_kernel(members, slots, key_ref, value_ref, column_slot_ref, *refs):
    query_refs, tab_refs, out_ref = refs[:members], refs[members : members + slots], refs[-1]
    rows = query_refs[0].shape[1]
    owner = jnp.concatenate([q[KEY_VALUE_HEADS, :, 0:1] for q in query_refs], axis=0)
    mine = owner.astype(jnp.float32) == column_slot_ref[0:1, :]
    ends = jnp.zeros((members * rows, HEAD_SIZE), jnp.float32)
    for h in range(KEY_VALUE_HEADS):
        at = head_lanes(h)
        query = jnp.concatenate([q[h] for q in query_refs], axis=0)
        tab_keys = jnp.concatenate([t[0, :, at] for t in tab_refs], axis=0)
        tab_values = jnp.concatenate([t[1, :, at] for t in tab_refs], axis=0)
        shared = lax.dot_general(query, key_ref[:, at], NT, preferred_element_type=jnp.float32)
        tab = lax.dot_general(query, tab_keys, NT, preferred_element_type=jnp.float32)
        tab = jnp.where(mine, tab * SCALE, FILLER)
        mean, end = block_softmax([shared * SCALE, tab], [value_ref[:, at], tab_values])
        for i in range(members):
            out_ref[i, h] = mean[i * rows : (i + 1) * rows]
        ends = put_lane(ends, h, end)
    for i in range(members):
        out_ref[i, KEY_VALUE_HEADS] = ends[i * rows : (i + 1) * rows]


def context_states(query_messages, keys, values, column_slot, tabs):
    members, rows = len(query_messages), query_messages[0].shape[1]
    key_count = keys.shape[0] + column_slot.shape[1]
    work = members * rows * KEY_VALUE_HEADS * key_count
    return pl.pallas_call(
        functools.partial(context_kernel, members, len(tabs)),
        out_shape=jax.ShapeDtypeStruct(
            (members, KEY_VALUE_HEADS + 1, rows, HEAD_SIZE), jnp.float32
        ),
        compiler_params=pltpu.CompilerParams(vmem_limit_bytes=VMEM_LIMIT),
        cost_estimate=pl.CostEstimate(
            flops=4 * work * HEAD_SIZE, transcendentals=work, bytes_accessed=4 * keys.size
        ),
        name="context_states",
    )(keys, values, column_slot, *query_messages, *tabs)


def suffix_kernel(steps, length_ref, query_ref, key_ref, value_ref, new_key_ref, new_value_ref, out_ref):
    rows, slots = query_ref.shape[1], key_ref.shape[0]
    used = lax.broadcasted_iota(jnp.int32, (rows, slots), 1) < length_ref[0]
    step = lax.rem(lax.broadcasted_iota(jnp.int32, (rows, steps), 0), steps)
    seen = lax.broadcasted_iota(jnp.int32, (rows, steps), 1) <= step
    ends = jnp.zeros((rows, HEAD_SIZE), jnp.float32)
    for h in range(KEY_VALUE_HEADS):
        at = head_lanes(h)
        query = query_ref[h]
        cached = lax.dot_general(query, key_ref[:, at], NT, preferred_element_type=jnp.float32)
        fresh = lax.dot_general(query, new_key_ref[:, at], NT, preferred_element_type=jnp.float32)
        cached = jnp.where(used, cached * SCALE, FILLER)
        fresh = jnp.where(seen, fresh * SCALE, FILLER)
        mean, end = block_softmax([cached, fresh], [value_ref[:, at], new_value_ref[:, at]])
        out_ref[h] = mean
        ends = put_lane(ends, h, end)
    out_ref[KEY_VALUE_HEADS] = ends


def suffix_state(query_message, cache_keys, cache_values, length, new_keys, new_values):
    rows, steps = query_message.shape[1], new_keys.shape[0]
    work = rows * KEY_VALUE_HEADS * cache_keys.shape[0]
    whole = pl.BlockSpec(memory_space=pltpu.VMEM)
    return pl.pallas_call(
        functools.partial(suffix_kernel, steps),
        in_specs=[pl.BlockSpec(memory_space=pltpu.SMEM)] + [whole] * 5,
        out_specs=whole,
        out_shape=jax.ShapeDtypeStruct((KEY_VALUE_HEADS + 1, rows, HEAD_SIZE), jnp.float32),
        compiler_params=pltpu.CompilerParams(vmem_limit_bytes=VMEM_LIMIT),
        cost_estimate=pl.CostEstimate(
            flops=4 * work * HEAD_SIZE, transcendentals=work, bytes_accessed=4 * cache_keys.size
        ),
        name="suffix_state",
    )(length, query_message, cache_keys, cache_values, new_keys, new_values)


def merge(parts):
    top = functools.reduce(jnp.maximum, [end for _, end in parts])
    shares = [jnp.exp(end - top) for _, end in parts]
    total = functools.reduce(jnp.add, shares)
    summed = functools.reduce(jnp.add, [mean * share for (mean, _), share in zip(parts, shares)])
    return summed / total, top + jnp.log(total)


def power(exponent):
    return jnp.exp2(exponent)


def pair_kernel(own_ref, other_ref, home_ref, *coded_refs):
    rows = own_ref.shape[2]
    for i in range(own_ref.shape[0]):
        slab = jnp.zeros((rows, HEAD_SIZE), jnp.float32)
        for h in range(KEY_VALUE_HEADS):
            mean, end = merge(
                [(r[i, h], r[i, KEY_VALUE_HEADS, :, h : h + 1]) for r in (own_ref, other_ref)]
            )
            if i == 0:
                home_ref[h] = mean
                slab = put_lane(slab, h, end)
                continue
            reach = jnp.max(jnp.abs(mean), axis=-1, keepdims=True)
            exponent = jnp.ceil(jnp.log2(jnp.maximum(reach, 1e-30)))
            code = jnp.round(mean * (power(-exponent) * CODE_TOP))
            coded_refs[i - 1][h] = code.astype(jnp.int32).astype(jnp.int16)
            near = jnp.round(end)
            slab = put_lane(slab, h, near)
            slab = put_lane(slab, KEY_VALUE_HEADS + h, jnp.round((end - near) * REST_TOP))
            slab = put_lane(slab, 2 * KEY_VALUE_HEADS + h, exponent)
        if i == 0:
            home_ref[KEY_VALUE_HEADS] = slab
        else:
            coded_refs[i - 1][KEY_VALUE_HEADS] = slab.astype(jnp.int32).astype(jnp.int16)


def pair_states(own, other):
    members, shape = own.shape[0], own.shape[1:]
    return pl.pallas_call(
        pair_kernel,
        out_shape=[jax.ShapeDtypeStruct(shape, jnp.float32)]
        + [jax.ShapeDtypeStruct(shape, jnp.int16)] * (members - 1),
        compiler_params=pltpu.CompilerParams(vmem_limit_bytes=VMEM_LIMIT),
        name="pair_states",
    )(own, other)


def final_kernel(suffix_ref, home_ref, *refs):
    coded_refs, out_ref = refs[:-1], refs[-1]
    steps = out_ref.shape[0]
    groups = suffix_ref.shape[1] // steps
    slabs = [r[KEY_VALUE_HEADS].astype(jnp.int32).astype(jnp.float32) for r in coded_refs]
    for h in range(KEY_VALUE_HEADS):
        parts = [(r[h], r[KEY_VALUE_HEADS, :, h : h + 1]) for r in (suffix_ref, home_ref)]
        for r, slab in zip(coded_refs, slabs):
            near, rest, exponent = (
                slab[:, k * KEY_VALUE_HEADS + h : k * KEY_VALUE_HEADS + h + 1] for k in range(3)
            )
            code = r[h].astype(jnp.int32).astype(jnp.float32)
            parts.append((code * (power(exponent) / CODE_TOP), near + rest / REST_TOP))
        mean, _ = merge(parts)
        for g in range(groups):
            out_ref[:, head_lanes(h * groups + g)] = mean[g * steps : (g + 1) * steps].astype(
                jnp.bfloat16
            )


def final_output(suffix, home, coded, steps):
    width = suffix.shape[1] // steps * KEY_VALUE_HEADS * HEAD_SIZE
    return pl.pallas_call(
        final_kernel,
        out_shape=jax.ShapeDtypeStruct((steps, width), jnp.bfloat16),
        compiler_params=pltpu.CompilerParams(vmem_limit_bytes=VMEM_LIMIT),
        name="final_output",
    )(suffix, home, *coded)


def swap(count, bit):
    return [(i, i ^ bit) for i in range(count)]


def shards(
    queries,
    prefix_key_value,
    tab_key_value,
    tab_owner,
    session_tab,
    suffix_key_value,
    suffix_len,
    token_keys,
    token_values,
):
    ctx_count, tab_count = lax.axis_size("ctx"), lax.axis_size("tab")
    pair_count = ctx_count // 2
    steps = queries.shape[1]
    tab_rows = tab_key_value.shape[1]

    tab_block = jnp.stack([tab_key_value[0, :, 0], tab_key_value[0, :, 1]])
    tabs = [tab_block] + [
        lax.ppermute(tab_block, "tab", swap(tab_count, k)) for k in range(1, tab_count)
    ]
    places = jnp.arange(tab_count * tab_rows, dtype=jnp.int32) // tab_rows
    column_slot = (places ^ lax.axis_index("tab")).astype(jnp.float32)[None]

    table = jnp.arange(tab_owner.shape[0], dtype=jnp.int32)
    slot = jnp.sum(jnp.where(session_tab[0] == table, tab_owner, 0))
    query = queries[0].reshape(steps, KEY_VALUE_HEADS, -1, HEAD_SIZE)
    query = query.transpose(1, 2, 0, 3).reshape(KEY_VALUE_HEADS, -1, HEAD_SIZE)
    slot_slab = jnp.broadcast_to(slot.astype(jnp.bfloat16), (1,) + query.shape[1:])
    message = jnp.concatenate([query, slot_slab], axis=0)
    column = [message] + [
        lax.ppermute(message, "ctx", swap(ctx_count, 2 * k)) for k in range(1, pair_count)
    ]
    other_column = [lax.ppermute(m, "ctx", swap(ctx_count, 1)) for m in column]

    keys, values = prefix_key_value[:, 0], prefix_key_value[:, 1]
    suffix = suffix_state(
        message,
        suffix_key_value[0, :, 0],
        suffix_key_value[0, :, 1],
        suffix_len,
        token_keys[0],
        token_values[0],
    )
    other = context_states(other_column, keys, values, column_slot, tabs)
    own = context_states(column, keys, values, column_slot, tabs)
    home, *coded = pair_states(own, lax.ppermute(other, "ctx", swap(ctx_count, 1)))
    received = [
        lax.ppermute(c, "ctx", swap(ctx_count, 2 * k)) for k, c in enumerate(coded, start=1)
    ]
    return final_output(suffix, home, received, steps)[None]


def solution(mesh):
    sessions = ("ctx", "tab")
    placed = (
        P(sessions, None, None),
        P("ctx", None, None),
        P("tab", "ctx", None, None),
        P(),
        P(sessions),
        P(sessions, None, None, None),
        P(sessions),
        P(sessions, None, None),
        P(sessions, None, None),
    )
    return jax.shard_map(
        shards, mesh=mesh, in_specs=placed, out_specs=P(sessions, None, None), check_vma=False
    )
```

```python
import functools

import jax
import jax.numpy as jnp
from jax import lax
from jax.experimental import pallas as pl
from jax.experimental.pallas import tpu as pltpu
from jax.sharding import PartitionSpec as P

KEY_VALUE_HEADS = 8
HEAD_SIZE = 128
SCALE = HEAD_SIZE**-0.5
SCALE_TWO = SCALE * 1.4426950408889634
MIB = 1024 * 1024
FILLER = -1e30
CODE_TOP = 32000.0
REST_TOP = 65000.0

NT = (((1,), (1,)), ((), ()))


def head_lanes(h):
    return pl.ds(h * HEAD_SIZE, HEAD_SIZE)


def put_lane(slab, lane, column):
    at = lax.broadcasted_iota(jnp.int32, slab.shape, 1)
    return jnp.where(at == lane, column, slab)


def vmem_limit(members, slots):
    return (16 if members * slots <= 32 else 48) * MIB


def in_any(count):
    return [pl.BlockSpec(memory_space=pl.ANY)] * count


def in_vmem(count):
    return [pl.BlockSpec(memory_space=pltpu.VMEM)] * count


def in_smem(count):
    return [pl.BlockSpec(memory_space=pltpu.SMEM)] * count


def prepare_kernel(tab_count, session_ref, owner_ref, query_ref, tab_ref, message_ref, block_ref):
    slot = jnp.int32(0)
    for k in range(tab_count):
        slot = jnp.where(session_ref[0] == k, owner_ref[k], slot)
    message_ref[:KEY_VALUE_HEADS] = query_ref[...]
    filled = jnp.full(message_ref.shape[1:], slot.astype(jnp.float32), jnp.float32)
    message_ref[KEY_VALUE_HEADS] = filled.astype(jnp.bfloat16)
    block_ref[0] = tab_ref[:, 0, :]
    block_ref[1] = tab_ref[:, 1, :]


def prepare(session_tab, tab_owner, query, tab):
    return pl.pallas_call(
        functools.partial(prepare_kernel, tab_owner.shape[0]),
        in_specs=in_smem(2) + in_vmem(2),
        out_shape=[
            jax.ShapeDtypeStruct((KEY_VALUE_HEADS + 1,) + query.shape[1:], jnp.bfloat16),
            jax.ShapeDtypeStruct((2, tab.shape[0], tab.shape[2]), jnp.bfloat16),
        ],
        compiler_params=pltpu.CompilerParams(vmem_limit_bytes=16 * MIB),
        name="prepare",
    )(session_tab, tab_owner, query, tab)


def split_kernel(paired_ref, key_ref, value_ref):
    key_ref[...] = paired_ref[:, 0, :]
    value_ref[...] = paired_ref[:, 1, :]


def split_pairs(paired):
    shape = jax.ShapeDtypeStruct((paired.shape[0], paired.shape[2]), paired.dtype)
    return pl.pallas_call(
        split_kernel,
        out_shape=[shape, shape],
        cost_estimate=pl.CostEstimate(
            flops=8 * paired.size, transcendentals=0, bytes_accessed=4 * paired.size
        ),
        compiler_params=pltpu.CompilerParams(vmem_limit_bytes=16 * MIB),
        name="split_pairs",
    )(paired)


def block_softmax(score_parts, value_parts):
    largest = functools.reduce(
        jnp.maximum, [jnp.max(s, axis=-1, keepdims=True) for s in score_parts]
    )
    product = 0.0
    for scores, values in zip(score_parts, value_parts):
        weights = jnp.exp2((scores - largest) * SCALE_TWO).astype(jnp.bfloat16)
        values = jnp.concatenate([values, jnp.ones_like(values)], axis=1)
        product += jnp.dot(weights, values, preferred_element_type=jnp.float32)
    summed, total = product[:, :HEAD_SIZE], product[:, HEAD_SIZE:]
    return summed / total, largest * SCALE + jnp.log(total)


def context_kernel(members, slots, after, key_ref, value_ref, column_slot_ref, *refs):
    query_refs, tab_refs, out_ref = refs[:members], refs[members : members + slots], refs[-1]
    rows = query_refs[0].shape[1]
    owner = jnp.concatenate([q[KEY_VALUE_HEADS, :, 0:1] for q in query_refs], axis=0)
    mine = owner.astype(jnp.float32) == column_slot_ref[0:1, :]
    ends = jnp.zeros((members * rows, HEAD_SIZE), jnp.float32)
    for h in range(KEY_VALUE_HEADS):
        at = head_lanes(h)
        query = jnp.concatenate([q[h] for q in query_refs], axis=0)
        tab_keys = jnp.concatenate([t[0, :, at] for t in tab_refs], axis=0)
        tab_values = jnp.concatenate([t[1, :, at] for t in tab_refs], axis=0)
        shared = lax.dot_general(query, key_ref[:, at], NT, preferred_element_type=jnp.float32)
        tab = lax.dot_general(query, tab_keys, NT, preferred_element_type=jnp.float32)
        tab = jnp.where(mine, tab, FILLER)
        mean, end = block_softmax([shared, tab], [value_ref[:, at], tab_values])
        for i in range(members):
            out_ref[i, h] = mean[i * rows : (i + 1) * rows]
        ends = put_lane(ends, h, end)
    for i in range(members):
        out_ref[i, KEY_VALUE_HEADS] = ends[i * rows : (i + 1) * rows]


def context_states(query_messages, keys, values, column_slot, tabs, after=()):
    members, rows = len(query_messages), query_messages[0].shape[1]
    key_count = keys.shape[0] + column_slot.shape[1]
    work = members * rows * KEY_VALUE_HEADS * key_count
    return pl.pallas_call(
        functools.partial(context_kernel, members, len(tabs), len(after)),
        in_specs=in_vmem(3 + members + len(tabs)) + in_any(len(after)),
        out_shape=jax.ShapeDtypeStruct(
            (members, KEY_VALUE_HEADS + 1, rows, HEAD_SIZE), jnp.float32
        ),
        compiler_params=pltpu.CompilerParams(vmem_limit_bytes=vmem_limit(members, len(tabs))),
        cost_estimate=pl.CostEstimate(
            flops=4 * work * HEAD_SIZE, transcendentals=work, bytes_accessed=4 * keys.size
        ),
        name="context_states",
    )(keys, values, column_slot, *query_messages, *tabs, *after)


def suffix_kernel(steps, length_ref, query_ref, pair_ref, new_key_ref, new_value_ref, *refs):
    out_ref = refs[-1]
    rows, slots = query_ref.shape[1], pair_ref.shape[0]
    used = lax.broadcasted_iota(jnp.int32, (rows, slots), 1) < length_ref[0]
    step = lax.rem(lax.broadcasted_iota(jnp.int32, (rows, steps), 0), steps)
    seen = lax.broadcasted_iota(jnp.int32, (rows, steps), 1) <= step
    ends = jnp.zeros((rows, HEAD_SIZE), jnp.float32)
    for h in range(KEY_VALUE_HEADS):
        at = head_lanes(h)
        query = query_ref[h]
        keys, values = pair_ref[:, 0, at], pair_ref[:, 1, at]
        cached = lax.dot_general(query, keys, NT, preferred_element_type=jnp.float32)
        fresh = lax.dot_general(query, new_key_ref[:, at], NT, preferred_element_type=jnp.float32)
        cached = jnp.where(used, cached, FILLER)
        fresh = jnp.where(seen, fresh, FILLER)
        mean, end = block_softmax([cached, fresh], [values, new_value_ref[:, at]])
        out_ref[h] = mean
        ends = put_lane(ends, h, end)
    out_ref[KEY_VALUE_HEADS] = ends


def suffix_state(query_message, cache, length, new_keys, new_values, after=()):
    rows, steps = query_message.shape[1], new_keys.shape[0]
    work = rows * KEY_VALUE_HEADS * cache.shape[0]
    return pl.pallas_call(
        functools.partial(suffix_kernel, steps),
        in_specs=in_smem(1) + in_vmem(4) + in_any(len(after)),
        out_shape=jax.ShapeDtypeStruct((KEY_VALUE_HEADS + 1, rows, HEAD_SIZE), jnp.float32),
        compiler_params=pltpu.CompilerParams(vmem_limit_bytes=16 * MIB),
        cost_estimate=pl.CostEstimate(
            flops=4 * work * HEAD_SIZE, transcendentals=work, bytes_accessed=4 * cache.size
        ),
        name="suffix_state",
    )(length, query_message, cache, new_keys, new_values, *after)


def shares_of(ends):
    top = functools.reduce(jnp.maximum, ends)
    shares = [jnp.exp(end - top) for end in ends]
    total = functools.reduce(jnp.add, shares)
    return [share / total for share in shares], top + jnp.log(total)


def mixed(parts, shares, h):
    return functools.reduce(
        jnp.add, [part * share[:, h : h + 1] for part, share in zip(parts, shares)]
    )


def pair_kernel(own_ref, other_ref, *coded_refs):
    rows = own_ref.shape[2]
    for i, coded_ref in enumerate(coded_refs):
        refs = (own_ref, other_ref)
        shares, end = shares_of([r[i, KEY_VALUE_HEADS] for r in refs])
        means = [mixed([r[i, h] for r in refs], shares, h) for h in range(KEY_VALUE_HEADS)]
        reach = jnp.ones((rows, HEAD_SIZE), jnp.float32)
        for h, mean in enumerate(means):
            reach = put_lane(reach, h, jnp.max(jnp.abs(mean), axis=-1, keepdims=True))
        exponent = jnp.ceil(jnp.log2(jnp.maximum(reach, 1e-30)))
        factor = jnp.exp2(-exponent) * CODE_TOP
        for h, mean in enumerate(means):
            code = jnp.round(mean * factor[:, h : h + 1])
            coded_ref[h] = code.astype(jnp.int32).astype(jnp.int16)
        near = jnp.round(end)
        rest = jnp.round((end - near) * REST_TOP)
        slab = jnp.zeros((rows, HEAD_SIZE), jnp.float32)
        for k, kind in enumerate((near, rest, exponent)):
            at = lax.broadcasted_iota(jnp.int32, slab.shape, 1)
            moved = pltpu.roll(kind, k * KEY_VALUE_HEADS, 1) if k else kind
            slab = jnp.where(at // KEY_VALUE_HEADS == k, moved, slab)
        coded_ref[KEY_VALUE_HEADS] = slab.astype(jnp.int32).astype(jnp.int16)


def pair_states(own, other):
    members, shape = own.shape[0], own.shape[1:]
    return pl.pallas_call(
        pair_kernel,
        out_shape=[jax.ShapeDtypeStruct(shape, jnp.int16)] * members,
        compiler_params=pltpu.CompilerParams(vmem_limit_bytes=16 * MIB),
        name="pair_states",
    )(own, other)


def final_kernel(suffix_ref, own_ref, other_ref, *refs):
    coded_refs, out_ref = refs[:-1], refs[-1]
    plain_refs = (suffix_ref, own_ref.at[0], other_ref.at[0])
    ends = [r[KEY_VALUE_HEADS] for r in plain_refs]
    factors = []
    for r in coded_refs:
        near = r[KEY_VALUE_HEADS].astype(jnp.int32).astype(jnp.float32)
        rest, exponent = (
            pltpu.roll(near, HEAD_SIZE - k * KEY_VALUE_HEADS, 1) for k in range(1, 3)
        )
        ends.append(near + rest / REST_TOP)
        factors.append(jnp.exp2(exponent) / CODE_TOP)
    head_lane = lax.broadcasted_iota(jnp.int32, ends[0].shape, 1) < KEY_VALUE_HEADS
    shares, _ = shares_of([jnp.where(head_lane, end, 0.0) for end in ends])
    for i, factor in enumerate(factors, start=len(plain_refs)):
        shares[i] = shares[i] * jnp.where(head_lane, factor, 0.0)
    for h in range(KEY_VALUE_HEADS):
        parts = [r[h] for r in plain_refs]
        parts += [r[h].astype(jnp.int32).astype(jnp.float32) for r in coded_refs]
        out_ref[h] = mixed(parts, shares, h).astype(jnp.bfloat16)


def final_output(suffix, own, other, coded):
    return pl.pallas_call(
        final_kernel,
        out_shape=jax.ShapeDtypeStruct((KEY_VALUE_HEADS,) + suffix.shape[1:], jnp.bfloat16),
        compiler_params=pltpu.CompilerParams(vmem_limit_bytes=16 * MIB),
        name="final_output",
    )(suffix, own, other, *coded)


def swap(count, bit):
    return [(i, i ^ bit) for i in range(count)]


def shards(
    queries,
    prefix_key_value,
    tab_key_value,
    tab_owner,
    session_tab,
    suffix_key_value,
    suffix_len,
    token_keys,
    token_values,
):
    ctx_count, tab_count = lax.axis_size("ctx"), lax.axis_size("tab")
    pair_count = ctx_count // 2
    steps = queries.shape[1]
    tab_rows = tab_key_value.shape[1]

    query = queries[0].reshape(steps, KEY_VALUE_HEADS, -1, HEAD_SIZE)
    query = query.transpose(1, 2, 0, 3).reshape(KEY_VALUE_HEADS, -1, HEAD_SIZE)
    message, tab_block = prepare(session_tab, tab_owner, query, tab_key_value[0])
    tabs = [tab_block] + [
        lax.ppermute(tab_block, "tab", swap(tab_count, k)) for k in range(1, tab_count)
    ]
    places = jnp.arange(tab_count * tab_rows, dtype=jnp.int32) // tab_rows
    column_slot = (places ^ lax.axis_index("tab")).astype(jnp.float32)[None]
    column = [message] + [
        lax.ppermute(message, "ctx", swap(ctx_count, 2 * k)) for k in range(1, pair_count)
    ]
    other_column = [lax.ppermute(m, "ctx", swap(ctx_count, 1)) for m in column]

    keys, values = split_pairs(prefix_key_value)
    shared = (keys, values, column_slot, tabs)
    other_far = context_states(other_column[1:], *shared)
    own_far = context_states(column[1:], *shared)
    coded = pair_states(own_far, lax.ppermute(other_far, "ctx", swap(ctx_count, 1)))
    received = [
        lax.ppermute(c, "ctx", swap(ctx_count, 2 * k)) for k, c in enumerate(coded, start=1)
    ]
    other_near = context_states(other_column[:1], *shared, after=coded[:1])
    own_near = context_states(column[:1], *shared, after=coded[:1])
    suffix = suffix_state(
        message, suffix_key_value[0], suffix_len, token_keys[0], token_values[0], after=coded[:1]
    )
    result = final_output(
        suffix, own_near, lax.ppermute(other_near, "ctx", swap(ctx_count, 1)), received
    )
    result = result.reshape(KEY_VALUE_HEADS, -1, steps, HEAD_SIZE)
    return result.transpose(2, 0, 1, 3).reshape(queries.shape)


def solution(mesh):
    sessions = ("ctx", "tab")
    placed = (
        P(sessions, None, None),
        P("ctx", None, None),
        P("tab", "ctx", None, None),
        P(),
        P(sessions),
        P(sessions, None, None, None),
        P(sessions),
        P(sessions, None, None),
        P(sessions, None, None),
    )
    return jax.shard_map(
        shards, mesh=mesh, in_specs=placed, out_specs=P(sessions, None, None), check_vma=False
    )
```

```python
import functools

import jax
import jax.numpy as jnp
from jax import lax
from jax.experimental import pallas as pl
from jax.experimental.pallas import tpu as pltpu
from jax.sharding import PartitionSpec as P

KEY_VALUE_HEADS = 8
HEAD_SIZE = 128
SCALE = HEAD_SIZE**-0.5
SCALE_TWO = SCALE * 1.4426950408889634
MIB = 1024 * 1024
FILLER = -1e30
CODE_TOP = 32000.0
REST_TOP = 65000.0

NT = (((1,), (1,)), ((), ()))


def head_lanes(h):
    return pl.ds(h * HEAD_SIZE, HEAD_SIZE)


def put_lane(slab, lane, column):
    at = lax.broadcasted_iota(jnp.int32, slab.shape, 1)
    return jnp.where(at == lane, column, slab)


def vmem_limit(members, slots):
    return (16 if members * slots <= 32 else 48) * MIB


def in_any(count):
    return [pl.BlockSpec(memory_space=pl.ANY)] * count


def in_hbm(count):
    return [pl.BlockSpec(memory_space=pltpu.HBM)] * count


def in_vmem(count):
    return [pl.BlockSpec(memory_space=pltpu.VMEM)] * count


def in_smem(count):
    return [pl.BlockSpec(memory_space=pltpu.SMEM)] * count


def prepare_kernel(
    session, owner_hbm, query_hbm, tab_hbm, message_ref, block_ref, paired, owner, sems
):
    moves = [
        (tab_hbm, paired),
        (owner_hbm, owner),
        (query_hbm, message_ref.at[pl.ds(0, KEY_VALUE_HEADS)]),
    ]
    copies = [pltpu.make_async_copy(*move, sems.at[i]) for i, move in enumerate(moves)]
    for copy in copies:
        copy.start()
    copies[1].wait()
    slot = jnp.int32(0)
    for k in range(owner.shape[0]):
        slot = jnp.where(session[0] == k, owner[k], slot)
    filled = jnp.full(message_ref.shape[1:], slot.astype(jnp.float32), jnp.float32)
    message_ref[KEY_VALUE_HEADS] = filled.astype(jnp.bfloat16)
    copies[0].wait()
    block_ref[0] = paired[:, 0, :]
    block_ref[1] = paired[:, 1, :]
    copies[2].wait()


def stay(arrays):
    return [pltpu.with_memory_space_constraint(array, pltpu.HBM) for array in arrays]


def prepare(session_tab, tab_owner, query, tab):
    return pl.pallas_call(
        prepare_kernel,
        in_specs=in_smem(1) + in_hbm(3),
        out_specs=in_vmem(2),
        out_shape=[
            jax.ShapeDtypeStruct((KEY_VALUE_HEADS + 1,) + query.shape[1:], jnp.bfloat16),
            jax.ShapeDtypeStruct((2, tab.shape[0], tab.shape[2]), jnp.bfloat16),
        ],
        scratch_shapes=[
            pltpu.VMEM(tab.shape, tab.dtype),
            pltpu.SMEM(tab_owner.shape, tab_owner.dtype),
            pltpu.SemaphoreType.DMA((4,)),
        ],
        compiler_params=pltpu.CompilerParams(vmem_limit_bytes=16 * MIB),
        name="prepare",
    )(session_tab, *stay([tab_owner, query, tab]))


def split_kernel(chunks, paired_ref, key_ref, value_ref, buffer, sems):
    rows = key_ref.shape[0] // chunks
    copies = [
        pltpu.make_async_copy(paired_ref.at[pl.ds(i * rows, rows)], buffer.at[i], sems.at[i])
        for i in range(chunks)
    ]
    for copy in copies:
        copy.start()
    for i, copy in enumerate(copies):
        copy.wait()
        key_ref[pl.ds(i * rows, rows)] = buffer[i, :, 0, :]
        value_ref[pl.ds(i * rows, rows)] = buffer[i, :, 1, :]


def split_pairs(paired, chunks=8):
    shape = jax.ShapeDtypeStruct((paired.shape[0], paired.shape[2]), paired.dtype)
    return pl.pallas_call(
        functools.partial(split_kernel, chunks),
        in_specs=in_hbm(1),
        out_specs=in_vmem(2),
        out_shape=[shape, shape],
        scratch_shapes=[
            pltpu.VMEM((chunks, paired.shape[0] // chunks) + paired.shape[1:], paired.dtype),
            pltpu.SemaphoreType.DMA((chunks,)),
        ],
        cost_estimate=pl.CostEstimate(
            flops=8 * paired.size, transcendentals=0, bytes_accessed=4 * paired.size
        ),
        compiler_params=pltpu.CompilerParams(vmem_limit_bytes=16 * MIB),
        name="split_pairs",
    )(*stay([paired]))


def block_softmax(score_parts, value_parts):
    largest = functools.reduce(
        jnp.maximum, [jnp.max(s, axis=-1, keepdims=True) for s in score_parts]
    )
    product = 0.0
    for scores, values in zip(score_parts, value_parts):
        weights = jnp.exp2((scores - largest) * SCALE_TWO).astype(jnp.bfloat16)
        values = jnp.concatenate([values, jnp.ones_like(values)], axis=1)
        product += jnp.dot(weights, values, preferred_element_type=jnp.float32)
    summed, total = product[:, :HEAD_SIZE], product[:, HEAD_SIZE:]
    return summed / total, largest * SCALE + jnp.log(total)


def context_kernel(members, slots, key_ref, value_ref, column_slot_ref, *refs):
    query_refs, tab_refs, out_ref = refs[:members], refs[members : members + slots], refs[-1]
    rows = query_refs[0].shape[1]
    owner = jnp.concatenate([q[KEY_VALUE_HEADS, :, 0:1] for q in query_refs], axis=0)
    mine = owner.astype(jnp.float32) == column_slot_ref[0:1, :]
    ends = jnp.zeros((members * rows, HEAD_SIZE), jnp.float32)
    for h in range(KEY_VALUE_HEADS):
        at = head_lanes(h)
        query = jnp.concatenate([q[h] for q in query_refs], axis=0)
        tab_keys = jnp.concatenate([t[0, :, at] for t in tab_refs], axis=0)
        tab_values = jnp.concatenate([t[1, :, at] for t in tab_refs], axis=0)
        shared = lax.dot_general(query, key_ref[:, at], NT, preferred_element_type=jnp.float32)
        tab = lax.dot_general(query, tab_keys, NT, preferred_element_type=jnp.float32)
        tab = jnp.where(mine, tab, FILLER)
        mean, end = block_softmax([shared, tab], [value_ref[:, at], tab_values])
        for i in range(members):
            out_ref[i, h] = mean[i * rows : (i + 1) * rows]
        ends = put_lane(ends, h, end)
    for i in range(members):
        out_ref[i, KEY_VALUE_HEADS] = ends[i * rows : (i + 1) * rows]


def context_states(query_messages, keys, values, column_slot, tabs):
    members, rows = len(query_messages), query_messages[0].shape[1]
    key_count = keys.shape[0] + column_slot.shape[1]
    work = members * rows * KEY_VALUE_HEADS * key_count
    return pl.pallas_call(
        functools.partial(context_kernel, members, len(tabs)),
        in_specs=in_vmem(3 + members + len(tabs)),
        out_shape=jax.ShapeDtypeStruct(
            (members, KEY_VALUE_HEADS + 1, rows, HEAD_SIZE), jnp.float32
        ),
        compiler_params=pltpu.CompilerParams(vmem_limit_bytes=vmem_limit(members, len(tabs))),
        cost_estimate=pl.CostEstimate(
            flops=4 * work * HEAD_SIZE, transcendentals=work, bytes_accessed=4 * keys.size
        ),
        name="context_states",
    )(keys, values, column_slot, *query_messages, *tabs)


def suffix_kernel(steps, length_ref, query_ref, pair_ref, new_key_ref, new_value_ref, *refs):
    out_ref = refs[-1]
    rows, slots = query_ref.shape[1], pair_ref.shape[0]
    used = lax.broadcasted_iota(jnp.int32, (rows, slots), 1) < length_ref[0]
    step = lax.rem(lax.broadcasted_iota(jnp.int32, (rows, steps), 0), steps)
    seen = lax.broadcasted_iota(jnp.int32, (rows, steps), 1) <= step
    ends = jnp.zeros((rows, HEAD_SIZE), jnp.float32)
    for h in range(KEY_VALUE_HEADS):
        at = head_lanes(h)
        query = query_ref[h]
        keys, values = pair_ref[:, 0, at], pair_ref[:, 1, at]
        cached = lax.dot_general(query, keys, NT, preferred_element_type=jnp.float32)
        fresh = lax.dot_general(query, new_key_ref[:, at], NT, preferred_element_type=jnp.float32)
        cached = jnp.where(used, cached, FILLER)
        fresh = jnp.where(seen, fresh, FILLER)
        mean, end = block_softmax([cached, fresh], [values, new_value_ref[:, at]])
        out_ref[h] = mean
        ends = put_lane(ends, h, end)
    out_ref[KEY_VALUE_HEADS] = ends


def suffix_state(query_message, cache, length, new_keys, new_values, after=()):
    rows, steps = query_message.shape[1], new_keys.shape[0]
    work = rows * KEY_VALUE_HEADS * cache.shape[0]
    return pl.pallas_call(
        functools.partial(suffix_kernel, steps),
        in_specs=in_smem(1) + in_vmem(4) + in_any(len(after)),
        out_shape=jax.ShapeDtypeStruct((KEY_VALUE_HEADS + 1, rows, HEAD_SIZE), jnp.float32),
        compiler_params=pltpu.CompilerParams(vmem_limit_bytes=16 * MIB),
        cost_estimate=pl.CostEstimate(
            flops=4 * work * HEAD_SIZE, transcendentals=work, bytes_accessed=4 * cache.size
        ),
        name="suffix_state",
    )(length, query_message, cache, new_keys, new_values, *after)


def shares_of(ends):
    top = functools.reduce(jnp.maximum, ends)
    shares = [jnp.exp(end - top) for end in ends]
    total = functools.reduce(jnp.add, shares)
    return [share / total for share in shares], top + jnp.log(total)


def mixed(parts, shares, h):
    return functools.reduce(
        jnp.add, [part * share[:, h : h + 1] for part, share in zip(parts, shares)]
    )


def pair_kernel(own_ref, other_ref, *coded_refs):
    rows = own_ref.shape[2]
    for i, coded_ref in enumerate(coded_refs):
        refs = (own_ref, other_ref)
        shares, end = shares_of([r[i, KEY_VALUE_HEADS] for r in refs])
        means = [mixed([r[i, h] for r in refs], shares, h) for h in range(KEY_VALUE_HEADS)]
        reach = jnp.ones((rows, HEAD_SIZE), jnp.float32)
        for h, mean in enumerate(means):
            reach = put_lane(reach, h, jnp.max(jnp.abs(mean), axis=-1, keepdims=True))
        exponent = jnp.ceil(jnp.log2(jnp.maximum(reach, 1e-30)))
        factor = jnp.exp2(-exponent) * CODE_TOP
        for h, mean in enumerate(means):
            code = jnp.round(mean * factor[:, h : h + 1])
            coded_ref[h] = code.astype(jnp.int32).astype(jnp.int16)
        near = jnp.round(end)
        rest = jnp.round((end - near) * REST_TOP)
        slab = jnp.zeros((rows, HEAD_SIZE), jnp.float32)
        for k, kind in enumerate((near, rest, exponent)):
            at = lax.broadcasted_iota(jnp.int32, slab.shape, 1)
            moved = pltpu.roll(kind, k * KEY_VALUE_HEADS, 1) if k else kind
            slab = jnp.where(at // KEY_VALUE_HEADS == k, moved, slab)
        coded_ref[KEY_VALUE_HEADS] = slab.astype(jnp.int32).astype(jnp.int16)


def pair_states(own, other):
    far, shape = own.shape[0] - 1, own.shape[1:]
    return pl.pallas_call(
        pair_kernel,
        out_shape=[jax.ShapeDtypeStruct(shape, jnp.int16)] * far,
        compiler_params=pltpu.CompilerParams(vmem_limit_bytes=16 * MIB),
        name="pair_states",
    )(own, other)


def final_kernel(suffix_ref, own_ref, other_ref, *refs):
    coded_refs, out_ref = refs[:-1], refs[-1]
    near = own_ref.shape[0] - 1
    plain_refs = (suffix_ref, own_ref.at[near], other_ref.at[near])
    ends = [r[KEY_VALUE_HEADS] for r in plain_refs]
    factors = []
    for r in coded_refs:
        near = r[KEY_VALUE_HEADS].astype(jnp.int32).astype(jnp.float32)
        rest, exponent = (
            pltpu.roll(near, HEAD_SIZE - k * KEY_VALUE_HEADS, 1) for k in range(1, 3)
        )
        ends.append(near + rest / REST_TOP)
        factors.append(jnp.exp2(exponent) / CODE_TOP)
    head_lane = lax.broadcasted_iota(jnp.int32, ends[0].shape, 1) < KEY_VALUE_HEADS
    shares, _ = shares_of([jnp.where(head_lane, end, 0.0) for end in ends])
    for i, factor in enumerate(factors, start=len(plain_refs)):
        shares[i] = shares[i] * jnp.where(head_lane, factor, 0.0)
    for h in range(KEY_VALUE_HEADS):
        parts = [r[h] for r in plain_refs]
        parts += [r[h].astype(jnp.int32).astype(jnp.float32) for r in coded_refs]
        out_ref[h] = mixed(parts, shares, h).astype(jnp.bfloat16)


def final_output(suffix, own, other, coded):
    return pl.pallas_call(
        final_kernel,
        out_shape=jax.ShapeDtypeStruct((KEY_VALUE_HEADS,) + suffix.shape[1:], jnp.bfloat16),
        compiler_params=pltpu.CompilerParams(vmem_limit_bytes=16 * MIB),
        name="final_output",
    )(suffix, own, other, *coded)


def swap(count, bit):
    return [(i, i ^ bit) for i in range(count)]


def shards(
    queries,
    prefix_key_value,
    tab_key_value,
    tab_owner,
    session_tab,
    suffix_key_value,
    suffix_len,
    token_keys,
    token_values,
):
    ctx_count, tab_count = lax.axis_size("ctx"), lax.axis_size("tab")
    pair_count = ctx_count // 2
    steps = queries.shape[1]
    tab_rows = tab_key_value.shape[1]

    query = queries[0].reshape(steps, KEY_VALUE_HEADS, -1, HEAD_SIZE)
    query = query.transpose(1, 2, 0, 3).reshape(KEY_VALUE_HEADS, -1, HEAD_SIZE)
    message, tab_block = prepare(session_tab, tab_owner, query, tab_key_value[0])
    tabs = [tab_block] + [
        lax.ppermute(tab_block, "tab", swap(tab_count, k)) for k in range(1, tab_count)
    ]
    far = [lax.ppermute(message, "ctx", swap(ctx_count, 2 * k)) for k in range(1, pair_count)]
    places = jnp.arange(tab_count * tab_rows, dtype=jnp.int32) // tab_rows
    column_slot = (places ^ lax.axis_index("tab")).astype(jnp.float32)[None]

    keys, values = split_pairs(prefix_key_value)
    far, keys = lax.optimization_barrier((far, keys))
    column = far + [message]
    other_column = [lax.ppermute(m, "ctx", swap(ctx_count, 1)) for m in column]
    theirs = context_states(other_column, keys, values, column_slot, tabs)
    ours = context_states(column, keys, values, column_slot, tabs)
    theirs = lax.ppermute(theirs, "ctx", swap(ctx_count, 1))
    coded = pair_states(ours, theirs)
    received = [
        lax.ppermute(c, "ctx", swap(ctx_count, 2 * k)) for k, c in enumerate(coded, start=1)
    ]
    suffix = suffix_state(
        message, suffix_key_value[0], suffix_len, token_keys[0], token_values[0], after=coded
    )
    result = final_output(suffix, ours, theirs, received)
    result = result.reshape(KEY_VALUE_HEADS, -1, steps, HEAD_SIZE)
    return result.transpose(2, 0, 1, 3).reshape(queries.shape)


def solution(mesh):
    sessions = ("ctx", "tab")
    placed = (
        P(sessions, None, None),
        P("ctx", None, None),
        P("tab", "ctx", None, None),
        P(),
        P(sessions),
        P(sessions, None, None, None),
        P(sessions),
        P(sessions, None, None),
        P(sessions, None, None),
    )
    return jax.shard_map(
        shards, mesh=mesh, in_specs=placed, out_specs=P(sessions, None, None), check_vma=False
    )
```

```python
import functools

import jax
import jax.numpy as jnp
from jax import lax
from jax.experimental import pallas as pl
from jax.experimental.pallas import tpu as pltpu
from jax.sharding import PartitionSpec as P

KEY_VALUE_HEADS = 8
HEAD_SIZE = 128
SCALE = HEAD_SIZE**-0.5
SCALE_TWO = SCALE * 1.4426950408889634
MIB = 1024 * 1024
FILLER = -1e30
CODE_TOP = 32000.0
REST_TOP = 65000.0

NT = (((1,), (1,)), ((), ()))


def head_lanes(h):
    return pl.ds(h * HEAD_SIZE, HEAD_SIZE)


def put_lane(slab, lane, column):
    at = lax.broadcasted_iota(jnp.int32, slab.shape, 1)
    return jnp.where(at == lane, column, slab)


def vmem_limit(members, slots=4):
    return (8 if members * slots <= 32 else 48) * MIB


def in_any(count):
    return [pl.BlockSpec(memory_space=pl.ANY)] * count


def in_hbm(count):
    return [pl.BlockSpec(memory_space=pltpu.HBM)] * count


def in_vmem(count):
    return [pl.BlockSpec(memory_space=pltpu.VMEM)] * count


def in_smem(count):
    return [pl.BlockSpec(memory_space=pltpu.SMEM)] * count


def tile_rows(paired):
    tiles = paired.reshape(paired.shape[0], 2, KEY_VALUE_HEADS, HEAD_SIZE)
    return tiles.transpose(0, 2, 1, 3).reshape(-1, HEAD_SIZE)


PER_ROW = 2 * KEY_VALUE_HEADS
EXTRA = 8


def split_rows(tiles, wide, first, count, key_ref, value_ref):
    start = first * PER_ROW
    wide[pl.ds(start, count * PER_ROW)] = tiles[pl.ds(start, count * PER_ROW)].astype(jnp.float32)
    for h in range(KEY_VALUE_HEADS):
        for k, ref in enumerate((key_ref, value_ref)):
            rows = wide[pl.ds(start + 2 * h + k, count, stride=PER_ROW), :]
            ref[pl.ds(first, count), head_lanes(h)] = rows.astype(ref.dtype)


def prepare_kernel(
    session, owner_hbm, query_hbm, tab_hbm, message_ref, block_ref, tiles, wide, owner, sems
):
    moves = [
        (tab_hbm, tiles),
        (owner_hbm, owner),
        (query_hbm, message_ref.at[0, pl.ds(0, query_hbm.shape[0])]),
    ]
    copies = [pltpu.make_async_copy(*move, sems.at[i]) for i, move in enumerate(moves)]
    for copy in copies:
        copy.start()
    copies[1].wait()
    slot = jnp.int32(0)
    for k in range(owner.shape[0]):
        slot = jnp.where(session[0] == k, owner[k], slot)
    filled = jnp.full((EXTRA, HEAD_SIZE), slot.astype(jnp.float32), jnp.float32)
    message_ref[0, pl.ds(query_hbm.shape[0], EXTRA)] = filled.astype(jnp.bfloat16)
    copies[0].wait()
    split_rows(tiles, wide, 0, block_ref.shape[1], block_ref.at[0], block_ref.at[1])
    copies[2].wait()


def stay(arrays):
    return [pltpu.with_memory_space_constraint(array, pltpu.HBM) for array in arrays]


def prepare(session_tab, tab_owner, query, tab):
    tiles = tile_rows(tab)
    return pl.pallas_call(
        prepare_kernel,
        in_specs=in_smem(1) + in_hbm(3),
        out_specs=in_vmem(2),
        out_shape=[
            jax.ShapeDtypeStruct((1, query.shape[0] + EXTRA, HEAD_SIZE), jnp.bfloat16),
            jax.ShapeDtypeStruct((2, tab.shape[0], tab.shape[2]), jnp.bfloat16),
        ],
        scratch_shapes=[
            pltpu.VMEM(tiles.shape, tiles.dtype),
            pltpu.VMEM(tiles.shape, jnp.float32),
            pltpu.SMEM(tab_owner.shape, tab_owner.dtype),
            pltpu.SemaphoreType.DMA((4,)),
        ],
        compiler_params=pltpu.CompilerParams(vmem_limit_bytes=6 * MIB),
        name="prepare",
    )(session_tab, *stay([tab_owner, query, tiles]))


def split_kernel(first, chunks, tiles_hbm, key_ref, value_ref, tiles, wide, sems):
    rows = key_ref.shape[0] // chunks
    piece = rows * PER_ROW
    copies = [
        pltpu.make_async_copy(
            tiles_hbm.at[pl.ds(first * PER_ROW + i * piece, piece)],
            tiles.at[pl.ds(i * piece, piece)],
            sems.at[i],
        )
        for i in range(chunks)
    ]
    for copy in copies:
        copy.start()
    for i, copy in enumerate(copies):
        copy.wait()
        split_rows(tiles, wide, i * rows, rows, key_ref, value_ref)


def split_pairs(tiles, first, rows, chunks=4):
    shape = jax.ShapeDtypeStruct((rows, KEY_VALUE_HEADS * HEAD_SIZE), tiles.dtype)
    scratch = (rows * PER_ROW, HEAD_SIZE)
    return pl.pallas_call(
        functools.partial(split_kernel, first, chunks),
        in_specs=in_hbm(1),
        out_specs=in_vmem(2),
        out_shape=[shape, shape],
        scratch_shapes=[
            pltpu.VMEM(scratch, tiles.dtype),
            pltpu.VMEM(scratch, jnp.float32),
            pltpu.SemaphoreType.DMA((chunks,)),
        ],
        compiler_params=pltpu.CompilerParams(vmem_limit_bytes=6 * MIB),
        name="split_pairs",
    )(*stay([tiles]))


def block_softmax(score_parts, value_parts):
    largest = functools.reduce(
        jnp.maximum, [jnp.max(s, axis=-1, keepdims=True) for s in score_parts]
    )
    product = 0.0
    for scores, values in zip(score_parts, value_parts):
        weights = jnp.exp2((scores - largest) * SCALE_TWO).astype(jnp.bfloat16)
        values = jnp.concatenate([values, jnp.ones_like(values)], axis=1)
        product += jnp.dot(weights, values, preferred_element_type=jnp.float32)
    summed, total = product[:, :HEAD_SIZE], product[:, HEAD_SIZE:]
    return summed / total, largest * SCALE + jnp.log(total)


def row_count(message):
    return (message.shape[-2] - EXTRA) // KEY_VALUE_HEADS


def rows_of(ref, h):
    rows = row_count(ref)
    return ref[pl.ds(h * rows, rows)]


def extra_of(ref):
    return ref[pl.ds(ref.shape[0] - EXTRA, EXTRA)]


def context_kernel(heads, sizes, pieces, shares, slots, column_slot_ref, *refs):
    query_refs = [r.at[i] for r in refs[:pieces] for i in range(r.shape[0])]
    refs = refs[pieces:]
    key_refs, value_refs, refs = refs[:shares], refs[shares : 2 * shares], refs[2 * shares :]
    tab_refs, out_refs, members = refs[:slots], refs[slots:], len(query_refs)
    places = [r.at[i] for r, size in zip(out_refs, sizes) for i in range(size)]
    rows = row_count(query_refs[0])
    owner = jnp.concatenate([extra_of(q)[:, 0:1] for q in query_refs for _ in range(rows // EXTRA)])
    mine = owner.astype(jnp.float32) == column_slot_ref[0:1, :]
    ends = jnp.zeros((members * rows, HEAD_SIZE), jnp.float32)
    for n, h in enumerate(heads):
        at = head_lanes(h)
        query = jnp.concatenate([rows_of(q, h) for q in query_refs], axis=0)
        tab_keys = jnp.concatenate([t[0, :, at] for t in tab_refs], axis=0)
        tab_values = jnp.concatenate([t[1, :, at] for t in tab_refs], axis=0)
        scores = [
            lax.dot_general(query, keys, NT, preferred_element_type=jnp.float32)
            for keys in [r[:, at] for r in key_refs] + [tab_keys]
        ]
        scores[-1] = jnp.where(mine, scores[-1], FILLER)
        mean, end = block_softmax(scores, [r[:, at] for r in value_refs] + [tab_values])
        for i, place in enumerate(places):
            place[n] = mean[i * rows : (i + 1) * rows]
        ends = put_lane(ends, h, end)
    for i, place in enumerate(places):
        place[len(heads)] = ends[i * rows : (i + 1) * rows]


def context_states(heads, sizes, pieces, keys, values, column_slot, tabs):
    members, rows = sum(sizes), row_count(pieces[0])
    key_count = sum(k.shape[0] for k in keys) + column_slot.shape[1]
    work = members * rows * len(heads) * key_count
    return pl.pallas_call(
        functools.partial(context_kernel, heads, sizes, len(pieces), len(keys), len(tabs)),
        in_specs=in_vmem(1 + len(pieces) + 2 * len(keys) + len(tabs)),
        out_specs=in_vmem(len(sizes)),
        out_shape=[
            jax.ShapeDtypeStruct((size, len(heads) + 1, rows, HEAD_SIZE), jnp.float32)
            for size in sizes
        ],
        compiler_params=pltpu.CompilerParams(vmem_limit_bytes=vmem_limit(members, len(tabs))),
        cost_estimate=pl.CostEstimate(
            flops=4 * work * HEAD_SIZE, transcendentals=work, bytes_accessed=1
        ),
        name="context_states",
    )(column_slot, *pieces, *keys, *values, *tabs)


def shares_of(ends):
    top = functools.reduce(jnp.maximum, ends)
    shares = [jnp.exp(end - top) for end in ends]
    total = functools.reduce(jnp.add, shares)
    return [share / total for share in shares], top + jnp.log(total)


def mixed(parts, shares, h):
    return functools.reduce(
        jnp.add, [part * share[:, h : h + 1] for part, share in zip(parts, shares)]
    )


def both_halves(i, low_ref, high_ref):
    halves = [r.at[i, h] for r in (low_ref, high_ref) for h in range(r.shape[1] - 1)]
    return halves, low_ref[i, low_ref.shape[1] - 1] + high_ref[i, high_ref.shape[1] - 1]


def home_kernel(
    steps, length_ref, query_ref, tiles, new_key_ref, new_value_ref, low_ref, high_ref, other_ref, *refs
):
    out_ref, wide, key_ref, value_ref = refs[-4:]
    rows, slots = row_count(query_ref), key_ref.shape[0]
    split_rows(tiles, wide, 0, slots, key_ref, value_ref)
    used = lax.broadcasted_iota(jnp.int32, (rows, slots), 1) < length_ref[0]
    step = lax.rem(lax.broadcasted_iota(jnp.int32, (rows, steps), 0), steps)
    seen = lax.broadcasted_iota(jnp.int32, (rows, steps), 1) <= step
    ends, means = jnp.zeros((rows, HEAD_SIZE), jnp.float32), []
    for h in range(KEY_VALUE_HEADS):
        at = head_lanes(h)
        query = rows_of(query_ref.at[0], h)
        cached = lax.dot_general(query, key_ref[:, at], NT, preferred_element_type=jnp.float32)
        fresh = lax.dot_general(query, new_key_ref[:, at], NT, preferred_element_type=jnp.float32)
        cached = jnp.where(used, cached, FILLER)
        fresh = jnp.where(seen, fresh, FILLER)
        mean, end = block_softmax([cached, fresh], [value_ref[:, at], new_value_ref[:, at]])
        means.append(mean)
        ends = put_lane(ends, h, end)
    own, own_end = both_halves(0, low_ref, high_ref)
    shares, end = shares_of([ends, own_end, other_ref[0, KEY_VALUE_HEADS]])
    for h, mean in enumerate(means):
        out_ref[h] = mixed([mean, own[h][...], other_ref[0, h]], shares, h)
    out_ref[KEY_VALUE_HEADS] = end


def home_state(query_message, cache, length, new_keys, new_values, low, high, other, after):
    rows, steps = row_count(query_message), new_keys.shape[0]
    work = rows * KEY_VALUE_HEADS * cache.shape[0]
    tiles = tile_rows(cache)
    return pl.pallas_call(
        functools.partial(home_kernel, steps),
        in_specs=in_smem(1) + in_vmem(7) + in_any(len(after)),
        out_shape=jax.ShapeDtypeStruct((KEY_VALUE_HEADS + 1, rows, HEAD_SIZE), jnp.float32),
        scratch_shapes=[
            pltpu.VMEM(tiles.shape, jnp.float32),
            pltpu.VMEM((cache.shape[0], cache.shape[2]), cache.dtype),
            pltpu.VMEM((cache.shape[0], cache.shape[2]), cache.dtype),
        ],
        compiler_params=pltpu.CompilerParams(vmem_limit_bytes=vmem_limit(low.shape[0])),
        cost_estimate=pl.CostEstimate(
            flops=4 * work * HEAD_SIZE, transcendentals=work, bytes_accessed=4 * cache.size
        ),
        name="home_state",
    )(length, query_message, tiles, new_keys, new_values, low, high, other, *after)


def pair_kernel(order, low_ref, high_ref, other_ref, *coded_refs):
    rows = other_ref.shape[2]
    for i, coded_ref in zip(order, coded_refs):
        own, own_end = both_halves(i, low_ref, high_ref)
        shares, end = shares_of([own_end, other_ref[i - 1, KEY_VALUE_HEADS]])
        means = [
            mixed([own[h][...], other_ref[i - 1, h]], shares, h) for h in range(KEY_VALUE_HEADS)
        ]
        reach = jnp.ones((rows, HEAD_SIZE), jnp.float32)
        for h, mean in enumerate(means):
            reach = put_lane(reach, h, jnp.max(jnp.abs(mean), axis=-1, keepdims=True))
        exponent = jnp.ceil(jnp.log2(jnp.maximum(reach, 1e-30)))
        factor = jnp.exp2(-exponent) * CODE_TOP
        for h, mean in enumerate(means):
            code = jnp.round(mean * factor[:, h : h + 1])
            coded_ref[pl.ds(h * rows, rows)] = code.astype(jnp.int32).astype(jnp.int16)
        near = jnp.round(end)
        rest = jnp.round((end - near) * REST_TOP)
        at = lax.broadcasted_iota(jnp.int32, (EXTRA, HEAD_SIZE), 1) // KEY_VALUE_HEADS
        slab, kinds = jnp.zeros((EXTRA, HEAD_SIZE), jnp.float32), (near, rest, exponent)
        for r in range(rows // EXTRA):
            for k, kind in enumerate(kinds):
                place = r * len(kinds) + k
                part = kind[r * EXTRA : (r + 1) * EXTRA]
                moved = pltpu.roll(part, place * KEY_VALUE_HEADS, 1) if place else part
                slab = jnp.where(at == place, moved, slab)
        coded_ref[pl.ds(KEY_VALUE_HEADS * rows, EXTRA)] = slab.astype(jnp.int32).astype(jnp.int16)


def pair_states(order, low, high, other):
    rows = other.shape[2]
    shape = (KEY_VALUE_HEADS * rows + EXTRA, HEAD_SIZE)
    return pl.pallas_call(
        functools.partial(pair_kernel, order),
        out_shape=[jax.ShapeDtypeStruct(shape, jnp.int16)] * len(order),
        compiler_params=pltpu.CompilerParams(vmem_limit_bytes=vmem_limit(low.shape[0])),
        name="pair_states",
    )(low, high, other)


def final_kernel(home_ref, *refs):
    coded_refs, out_ref = refs[:-1], refs[-1]
    rows = home_ref.shape[1]
    ends, factors = [home_ref[KEY_VALUE_HEADS]], []
    head_lane = lax.broadcasted_iota(jnp.int32, ends[0].shape, 1) < KEY_VALUE_HEADS
    for r in coded_refs:
        slab = extra_of(r).astype(jnp.int32).astype(jnp.float32)
        near, rest, exponent = (
            jnp.concatenate(
                [
                    pltpu.roll(slab, (HEAD_SIZE - (3 * i + k) * KEY_VALUE_HEADS) % HEAD_SIZE, 1)
                    for i in range(rows // EXTRA)
                ]
            )
            for k in range(3)
        )
        ends.append(near + rest / REST_TOP)
        factors.append(jnp.exp2(jnp.where(head_lane, exponent, 0.0)) / CODE_TOP)
    shares, _ = shares_of([jnp.where(head_lane, end, 0.0) for end in ends])
    shares = shares[:1] + [share * factor for share, factor in zip(shares[1:], factors)]
    for h in range(KEY_VALUE_HEADS):
        parts = [rows_of(r, h).astype(jnp.int32).astype(jnp.float32) for r in coded_refs]
        out_ref[h] = mixed([home_ref[h]] + parts, shares, h).astype(jnp.bfloat16)


def final_output(home, coded):
    return pl.pallas_call(
        final_kernel,
        out_shape=jax.ShapeDtypeStruct((KEY_VALUE_HEADS,) + home.shape[1:], jnp.bfloat16),
        compiler_params=pltpu.CompilerParams(vmem_limit_bytes=vmem_limit(len(coded))),
        name="final_output",
    )(home, *coded)


def swap(count, bit):
    return [(i, i ^ bit) for i in range(count)]


def shards(
    queries,
    prefix_key_value,
    tab_key_value,
    tab_owner,
    session_tab,
    suffix_key_value,
    suffix_len,
    token_keys,
    token_values,
):
    ctx_count, tab_count = lax.axis_size("ctx"), lax.axis_size("tab")
    pair_count = ctx_count // 2
    steps = queries.shape[1]
    tab_rows = tab_key_value.shape[1]

    query = queries[0].reshape(steps, KEY_VALUE_HEADS, -1, HEAD_SIZE)
    query = query.transpose(1, 2, 0, 3).reshape(-1, HEAD_SIZE)
    message, tab_block = prepare(session_tab, tab_owner, query, tab_key_value[0])
    tabs = [tab_block] + [
        lax.ppermute(tab_block, "tab", swap(tab_count, k)) for k in range(1, tab_count)
    ]
    places = jnp.arange(tab_count * tab_rows, dtype=jnp.int32) // tab_rows
    column_slot = (places ^ lax.axis_index("tab")).astype(jnp.float32)[None]

    tiles = tile_rows(prefix_key_value)
    half = prefix_key_value.shape[0] // 2
    splits = [split_pairs(tiles, i * half, half) for i in range(2)]
    pieces, masks, bit = [message], [0], pair_count // 2
    while bit:
        if len(masks) == 2:
            pieces[-1], splits[0] = lax.optimization_barrier((pieces[-1], splits[0]))
        column = jnp.concatenate(pieces, axis=0) if len(pieces) > 1 else message
        pieces = [column, lax.ppermute(column, "ctx", swap(ctx_count, 2 * bit))]
        masks, bit = masks + [mask ^ bit for mask in masks], bit // 2
    pieces[-1], tabs, splits = lax.optimization_barrier((pieces[-1], tabs, splits))
    other_pieces = [lax.ppermute(piece, "ctx", swap(ctx_count, 1)) for piece in pieces]
    keys, values = zip(*splits)
    shared = (keys, values, column_slot, tabs)
    heads = tuple(range(KEY_VALUE_HEADS))
    first, second = heads[: len(heads) // 2], heads[len(heads) // 2 :]
    (low,) = context_states(first, (pair_count,), pieces, *shared)
    other_pieces, low = lax.optimization_barrier((other_pieces, low))
    near, far = context_states(heads, (1, pair_count - 1), other_pieces, *shared)
    pieces, far = lax.optimization_barrier((pieces, far))
    far = lax.ppermute(far, "ctx", swap(ctx_count, 1))
    near = lax.ppermute(near, "ctx", swap(ctx_count, 1))
    (high,) = context_states(second, (pair_count,), pieces, *shared)
    order = sorted(range(1, pair_count), key=lambda i: masks[i])
    coded = pair_states(order, low, high, far)
    received = [
        lax.ppermute(code, "ctx", swap(ctx_count, 2 * masks[i])) for i, code in zip(order, coded)
    ]
    home = home_state(
        message,
        suffix_key_value[0],
        suffix_len,
        token_keys[0],
        token_values[0],
        low,
        high,
        near,
        after=coded,
    )
    result = final_output(home, received)
    result = result.reshape(KEY_VALUE_HEADS, -1, steps, HEAD_SIZE)
    return result.transpose(2, 0, 1, 3).reshape(queries.shape)


def solution(mesh):
    sessions = ("ctx", "tab")
    placed = (
        P(sessions, None, None),
        P("ctx", None, None),
        P("tab", "ctx", None, None),
        P(),
        P(sessions),
        P(sessions, None, None, None),
        P(sessions),
        P(sessions, None, None),
        P(sessions, None, None),
    )
    return jax.shard_map(
        shards, mesh=mesh, in_specs=placed, out_specs=P(sessions, None, None), check_vma=False
    )
```

```python
import functools

import jax
import jax.numpy as jnp
from jax import lax
from jax.experimental import pallas as pl
from jax.experimental.pallas import tpu as pltpu
from jax.sharding import PartitionSpec as P

KEY_VALUE_HEADS = 8
HEAD_SIZE = 128
SCALE = HEAD_SIZE**-0.5
SCALE_TWO = SCALE * 1.4426950408889634
MIB = 1024 * 1024
FILLER = -1e30
CODE_TOP = 32000.0
REST_TOP = 65000.0

NT = (((1,), (1,)), ((), ()))


def head_lanes(h):
    return pl.ds(h * HEAD_SIZE, HEAD_SIZE)


def put_lane(slab, lane, column):
    at = lax.broadcasted_iota(jnp.int32, slab.shape, 1)
    return jnp.where(at == lane, column, slab)


def vmem_limit(members, slots=4):
    return (8 if members * slots <= 32 else 48) * MIB


def in_any(count):
    return [pl.BlockSpec(memory_space=pl.ANY)] * count


def in_hbm(count):
    return [pl.BlockSpec(memory_space=pltpu.HBM)] * count


def in_vmem(count):
    return [pl.BlockSpec(memory_space=pltpu.VMEM)] * count


def in_smem(count):
    return [pl.BlockSpec(memory_space=pltpu.SMEM)] * count


def tile_rows(paired):
    tiles = paired.reshape(paired.shape[0], 2, KEY_VALUE_HEADS, HEAD_SIZE)
    return tiles.transpose(0, 2, 1, 3).reshape(-1, HEAD_SIZE)


PER_ROW = 2 * KEY_VALUE_HEADS
EXTRA = 8


def split_rows(tiles, wide, first, count, key_ref, value_ref):
    start = first * PER_ROW
    wide[pl.ds(start, count * PER_ROW)] = tiles[pl.ds(start, count * PER_ROW)].astype(jnp.float32)
    for h in range(KEY_VALUE_HEADS):
        for k, ref in enumerate((key_ref, value_ref)):
            rows = wide[pl.ds(start + 2 * h + k, count, stride=PER_ROW), :]
            ref[pl.ds(first, count), head_lanes(h)] = rows.astype(ref.dtype)


def prepare_kernel(
    session, owner_hbm, query_hbm, tab_hbm, message_ref, block_ref, tiles, wide, owner, sems
):
    moves = [
        (tab_hbm, tiles),
        (owner_hbm, owner),
        (query_hbm, message_ref.at[0, pl.ds(0, query_hbm.shape[0])]),
    ]
    copies = [pltpu.make_async_copy(*move, sems.at[i]) for i, move in enumerate(moves)]
    for copy in copies:
        copy.start()
    copies[1].wait()
    slot = jnp.int32(0)
    for k in range(owner.shape[0]):
        slot = jnp.where(session[0] == k, owner[k], slot)
    filled = jnp.full((EXTRA, HEAD_SIZE), slot.astype(jnp.float32), jnp.float32)
    message_ref[0, pl.ds(query_hbm.shape[0], EXTRA)] = filled.astype(jnp.bfloat16)
    copies[0].wait()
    split_rows(tiles, wide, 0, block_ref.shape[1], block_ref.at[0], block_ref.at[1])
    copies[2].wait()


def stay(arrays):
    return [pltpu.with_memory_space_constraint(array, pltpu.HBM) for array in arrays]


def prepare(session_tab, tab_owner, query, tab):
    tiles = tile_rows(tab)
    return pl.pallas_call(
        prepare_kernel,
        in_specs=in_smem(1) + in_hbm(3),
        out_specs=in_vmem(2),
        out_shape=[
            jax.ShapeDtypeStruct((1, query.shape[0] + EXTRA, HEAD_SIZE), jnp.bfloat16),
            jax.ShapeDtypeStruct((2, tab.shape[0], tab.shape[2]), jnp.bfloat16),
        ],
        scratch_shapes=[
            pltpu.VMEM(tiles.shape, tiles.dtype),
            pltpu.VMEM(tiles.shape, jnp.float32),
            pltpu.SMEM(tab_owner.shape, tab_owner.dtype),
            pltpu.SemaphoreType.DMA((4,)),
        ],
        compiler_params=pltpu.CompilerParams(vmem_limit_bytes=6 * MIB),
        name="prepare",
    )(session_tab, *stay([tab_owner, query, tiles]))


def split_kernel(first, chunks, tiles_hbm, key_ref, value_ref, tiles, wide, sems):
    rows = key_ref.shape[0] // chunks
    piece = rows * PER_ROW
    copies = [
        pltpu.make_async_copy(
            tiles_hbm.at[pl.ds(first * PER_ROW + i * piece, piece)],
            tiles.at[pl.ds(i * piece, piece)],
            sems.at[i],
        )
        for i in range(chunks)
    ]
    for copy in copies:
        copy.start()
    for i, copy in enumerate(copies):
        copy.wait()
        split_rows(tiles, wide, i * rows, rows, key_ref, value_ref)


def split_pairs(tiles, first, rows, chunks=4):
    shape = jax.ShapeDtypeStruct((rows, KEY_VALUE_HEADS * HEAD_SIZE), tiles.dtype)
    scratch = (rows * PER_ROW, HEAD_SIZE)
    return pl.pallas_call(
        functools.partial(split_kernel, first, chunks),
        in_specs=in_hbm(1),
        out_specs=in_vmem(2),
        out_shape=[shape, shape],
        scratch_shapes=[
            pltpu.VMEM(scratch, tiles.dtype),
            pltpu.VMEM(scratch, jnp.float32),
            pltpu.SemaphoreType.DMA((chunks,)),
        ],
        compiler_params=pltpu.CompilerParams(vmem_limit_bytes=6 * MIB),
        name="split_pairs",
    )(*stay([tiles]))


def block_softmax(score_parts, value_parts):
    largest = functools.reduce(
        jnp.maximum, [jnp.max(s, axis=-1, keepdims=True) for s in score_parts]
    )
    product = 0.0
    for scores, values in zip(score_parts, value_parts):
        weights = jnp.exp2((scores - largest) * SCALE_TWO).astype(jnp.bfloat16)
        values = jnp.concatenate([values, jnp.ones_like(values)], axis=1)
        product += jnp.dot(weights, values, preferred_element_type=jnp.float32)
    summed, total = product[:, :HEAD_SIZE], product[:, HEAD_SIZE:]
    return summed / total, largest * SCALE + jnp.log(total)


def row_count(message):
    return (message.shape[-2] - EXTRA) // KEY_VALUE_HEADS


def rows_of(ref, h):
    rows = row_count(ref)
    return ref[pl.ds(h * rows, rows)]


def extra_of(ref):
    return ref[pl.ds(ref.shape[0] - EXTRA, EXTRA)]


def context_kernel(heads, sizes, pieces, shares, slots, column_slot_ref, *refs):
    query_refs = [r.at[i] for r in refs[:pieces] for i in range(r.shape[0])]
    refs = refs[pieces:]
    key_refs, value_refs, refs = refs[:shares], refs[shares : 2 * shares], refs[2 * shares :]
    tab_refs, out_refs, members = refs[:slots], refs[slots:], len(query_refs)
    places = [r.at[i] for r, size in zip(out_refs, sizes) for i in range(size)]
    rows = row_count(query_refs[0])
    owner = jnp.concatenate([extra_of(q)[:, 0:1] for q in query_refs for _ in range(rows // EXTRA)])
    mine = owner.astype(jnp.float32) == column_slot_ref[0:1, :]
    ends = jnp.zeros((members * rows, HEAD_SIZE), jnp.float32)
    for n, h in enumerate(heads):
        at = head_lanes(h)
        query = jnp.concatenate([rows_of(q, h) for q in query_refs], axis=0)
        tab_keys = jnp.concatenate([t[0, :, at] for t in tab_refs], axis=0)
        tab_values = jnp.concatenate([t[1, :, at] for t in tab_refs], axis=0)
        scores = [
            lax.dot_general(query, keys, NT, preferred_element_type=jnp.float32)
            for keys in [r[:, at] for r in key_refs] + [tab_keys]
        ]
        scores[-1] = jnp.where(mine, scores[-1], FILLER)
        mean, end = block_softmax(scores, [r[:, at] for r in value_refs] + [tab_values])
        for i, place in enumerate(places):
            place[n] = mean[i * rows : (i + 1) * rows]
        ends = put_lane(ends, h, end)
    for i, place in enumerate(places):
        place[len(heads)] = ends[i * rows : (i + 1) * rows]


def context_states(heads, sizes, pieces, keys, values, column_slot, tabs):
    members, rows = sum(sizes), row_count(pieces[0])
    key_count = sum(k.shape[0] for k in keys) + column_slot.shape[1]
    work = members * rows * len(heads) * key_count
    return pl.pallas_call(
        functools.partial(context_kernel, heads, sizes, len(pieces), len(keys), len(tabs)),
        in_specs=in_vmem(1 + len(pieces) + 2 * len(keys) + len(tabs)),
        out_specs=in_vmem(len(sizes)),
        out_shape=[
            jax.ShapeDtypeStruct((size, len(heads) + 1, rows, HEAD_SIZE), jnp.float32)
            for size in sizes
        ],
        compiler_params=pltpu.CompilerParams(vmem_limit_bytes=vmem_limit(members, len(tabs))),
        cost_estimate=pl.CostEstimate(
            flops=4 * work * HEAD_SIZE, transcendentals=work, bytes_accessed=1
        ),
        name="context_states",
    )(column_slot, *pieces, *keys, *values, *tabs)


def shares_of(ends):
    top = functools.reduce(jnp.maximum, ends)
    shares = [jnp.exp(end - top) for end in ends]
    total = functools.reduce(jnp.add, shares)
    return [share / total for share in shares], top + jnp.log(total)


def mixed(parts, shares, h):
    return functools.reduce(
        jnp.add, [part * share[:, h : h + 1] for part, share in zip(parts, shares)]
    )


def both_halves(i, low_ref, high_ref):
    halves = [r.at[i, h] for r in (low_ref, high_ref) for h in range(r.shape[1] - 1)]
    return halves, low_ref[i, low_ref.shape[1] - 1] + high_ref[i, high_ref.shape[1] - 1]


def home_kernel(
    steps, length_ref, query_ref, tiles, new_key_ref, new_value_ref, low_ref, high_ref, other_ref, *refs
):
    out_ref, wide, key_ref, value_ref = refs[-4:]
    rows, slots = row_count(query_ref), key_ref.shape[0]
    split_rows(tiles, wide, 0, slots, key_ref, value_ref)
    used = lax.broadcasted_iota(jnp.int32, (rows, slots), 1) < length_ref[0]
    step = lax.rem(lax.broadcasted_iota(jnp.int32, (rows, steps), 0), steps)
    seen = lax.broadcasted_iota(jnp.int32, (rows, steps), 1) <= step
    ends, means = jnp.zeros((rows, HEAD_SIZE), jnp.float32), []
    for h in range(KEY_VALUE_HEADS):
        at = head_lanes(h)
        query = rows_of(query_ref.at[0], h)
        cached = lax.dot_general(query, key_ref[:, at], NT, preferred_element_type=jnp.float32)
        fresh = lax.dot_general(query, new_key_ref[:, at], NT, preferred_element_type=jnp.float32)
        cached = jnp.where(used, cached, FILLER)
        fresh = jnp.where(seen, fresh, FILLER)
        mean, end = block_softmax([cached, fresh], [value_ref[:, at], new_value_ref[:, at]])
        means.append(mean)
        ends = put_lane(ends, h, end)
    own, own_end = both_halves(0, low_ref, high_ref)
    shares, end = shares_of([ends, own_end, other_ref[0, KEY_VALUE_HEADS]])
    for h, mean in enumerate(means):
        out_ref[h] = mixed([mean, own[h][...], other_ref[0, h]], shares, h)
    out_ref[KEY_VALUE_HEADS] = end


def home_state(query_message, cache, length, new_keys, new_values, low, high, other, after):
    rows, steps = row_count(query_message), new_keys.shape[0]
    work = rows * KEY_VALUE_HEADS * cache.shape[0]
    tiles = tile_rows(cache)
    return pl.pallas_call(
        functools.partial(home_kernel, steps),
        in_specs=in_smem(1) + in_vmem(7) + in_any(len(after)),
        out_shape=jax.ShapeDtypeStruct((KEY_VALUE_HEADS + 1, rows, HEAD_SIZE), jnp.float32),
        scratch_shapes=[
            pltpu.VMEM(tiles.shape, jnp.float32),
            pltpu.VMEM((cache.shape[0], cache.shape[2]), cache.dtype),
            pltpu.VMEM((cache.shape[0], cache.shape[2]), cache.dtype),
        ],
        compiler_params=pltpu.CompilerParams(vmem_limit_bytes=vmem_limit(low.shape[0])),
        cost_estimate=pl.CostEstimate(
            flops=4 * work * HEAD_SIZE, transcendentals=work, bytes_accessed=4 * cache.size
        ),
        name="home_state",
    )(length, query_message, tiles, new_keys, new_values, low, high, other, *after)


def pair_kernel(order, low_ref, high_ref, other_ref, *coded_refs):
    rows = other_ref.shape[2]
    for i, coded_ref in zip(order, coded_refs):
        own, own_end = both_halves(i, low_ref, high_ref)
        shares, end = shares_of([own_end, other_ref[i - 1, KEY_VALUE_HEADS]])
        means = [
            mixed([own[h][...], other_ref[i - 1, h]], shares, h) for h in range(KEY_VALUE_HEADS)
        ]
        reach = jnp.ones((rows, HEAD_SIZE), jnp.float32)
        for h, mean in enumerate(means):
            reach = put_lane(reach, h, jnp.max(jnp.abs(mean), axis=-1, keepdims=True))
        exponent = jnp.ceil(jnp.log2(jnp.maximum(reach, 1e-30)))
        factor = jnp.exp2(-exponent) * CODE_TOP
        for h, mean in enumerate(means):
            code = jnp.round(mean * factor[:, h : h + 1])
            coded_ref[pl.ds(h * rows, rows)] = code.astype(jnp.int32).astype(jnp.int16)
        near = jnp.round(end)
        rest = jnp.round((end - near) * REST_TOP)
        at = lax.broadcasted_iota(jnp.int32, (EXTRA, HEAD_SIZE), 1) // KEY_VALUE_HEADS
        slab, kinds = jnp.zeros((EXTRA, HEAD_SIZE), jnp.float32), (near, rest, exponent)
        for r in range(rows // EXTRA):
            for k, kind in enumerate(kinds):
                place = r * len(kinds) + k
                part = kind[r * EXTRA : (r + 1) * EXTRA]
                moved = pltpu.roll(part, place * KEY_VALUE_HEADS, 1) if place else part
                slab = jnp.where(at == place, moved, slab)
        coded_ref[pl.ds(KEY_VALUE_HEADS * rows, EXTRA)] = slab.astype(jnp.int32).astype(jnp.int16)


def pair_states(order, low, high, other):
    rows = other.shape[2]
    shape = (KEY_VALUE_HEADS * rows + EXTRA, HEAD_SIZE)
    return pl.pallas_call(
        functools.partial(pair_kernel, order),
        out_shape=[jax.ShapeDtypeStruct(shape, jnp.int16)] * len(order),
        compiler_params=pltpu.CompilerParams(vmem_limit_bytes=vmem_limit(low.shape[0])),
        name="pair_states",
    )(low, high, other)


def final_kernel(home_ref, *refs):
    coded_refs, out_ref = refs[:-1], refs[-1]
    rows = home_ref.shape[1]
    ends, factors = [home_ref[KEY_VALUE_HEADS]], []
    head_lane = lax.broadcasted_iota(jnp.int32, ends[0].shape, 1) < KEY_VALUE_HEADS
    for r in coded_refs:
        slab = extra_of(r).astype(jnp.int32).astype(jnp.float32)
        near, rest, exponent = (
            jnp.concatenate(
                [
                    pltpu.roll(slab, (HEAD_SIZE - (3 * i + k) * KEY_VALUE_HEADS) % HEAD_SIZE, 1)
                    for i in range(rows // EXTRA)
                ]
            )
            for k in range(3)
        )
        ends.append(near + rest / REST_TOP)
        factors.append(jnp.exp2(jnp.where(head_lane, exponent, 0.0)) / CODE_TOP)
    shares, _ = shares_of([jnp.where(head_lane, end, 0.0) for end in ends])
    shares = shares[:1] + [share * factor for share, factor in zip(shares[1:], factors)]
    for h in range(KEY_VALUE_HEADS):
        parts = [rows_of(r, h).astype(jnp.int32).astype(jnp.float32) for r in coded_refs]
        out_ref[h] = mixed([home_ref[h]] + parts, shares, h).astype(jnp.bfloat16)


def final_output(home, coded):
    return pl.pallas_call(
        final_kernel,
        out_shape=jax.ShapeDtypeStruct((KEY_VALUE_HEADS,) + home.shape[1:], jnp.bfloat16),
        compiler_params=pltpu.CompilerParams(vmem_limit_bytes=vmem_limit(len(coded))),
        name="final_output",
    )(home, *coded)


def swap(count, bit):
    return [(i, i ^ bit) for i in range(count)]


def shards(
    queries,
    prefix_key_value,
    tab_key_value,
    tab_owner,
    session_tab,
    suffix_key_value,
    suffix_len,
    token_keys,
    token_values,
):
    ctx_count, tab_count = lax.axis_size("ctx"), lax.axis_size("tab")
    pair_count = ctx_count // 2
    steps = queries.shape[1]
    tab_rows = tab_key_value.shape[1]

    query = queries[0].reshape(steps, KEY_VALUE_HEADS, -1, HEAD_SIZE)
    query = query.transpose(1, 2, 0, 3).reshape(-1, HEAD_SIZE)
    message, tab_block = prepare(session_tab, tab_owner, query, tab_key_value[0])
    tabs = [tab_block] + [
        lax.ppermute(tab_block, "tab", swap(tab_count, k)) for k in range(1, tab_count)
    ]
    places = jnp.arange(tab_count * tab_rows, dtype=jnp.int32) // tab_rows
    column_slot = (places ^ lax.axis_index("tab")).astype(jnp.float32)[None]

    tiles = tile_rows(prefix_key_value)
    half = prefix_key_value.shape[0] // 2
    splits = [split_pairs(tiles, i * half, half) for i in range(2)]
    pieces, masks, bit = [message], [0], pair_count // 2
    while bit:
        if len(masks) == 2:
            pieces[-1], splits[0] = lax.optimization_barrier((pieces[-1], splits[0]))
        column = jnp.concatenate(pieces, axis=0) if len(pieces) > 1 else message
        pieces = [column, lax.ppermute(column, "ctx", swap(ctx_count, 2 * bit))]
        masks, bit = masks + [mask ^ bit for mask in masks], bit // 2
    pieces[-1], tabs, splits = lax.optimization_barrier((pieces[-1], tabs, splits))
    other_pieces = [lax.ppermute(piece, "ctx", swap(ctx_count, 1)) for piece in pieces]
    keys, values = zip(*splits)
    shared = (keys, values, column_slot, tabs)
    heads = tuple(range(KEY_VALUE_HEADS))
    first, second = heads[:5], heads[5:]
    (low,) = context_states(first, (pair_count,), pieces, *shared)
    other_pieces, low = lax.optimization_barrier((other_pieces, low))
    near, far = context_states(heads, (1, pair_count - 1), other_pieces, *shared)
    pieces, far = lax.optimization_barrier((pieces, far))
    far = lax.ppermute(far, "ctx", swap(ctx_count, 1))
    near = lax.ppermute(near, "ctx", swap(ctx_count, 1))
    (high,) = context_states(second, (pair_count,), pieces, *shared)
    order = sorted(range(1, pair_count), key=lambda i: masks[i])
    coded = pair_states(order, low, high, far)
    received = [
        lax.ppermute(code, "ctx", swap(ctx_count, 2 * masks[i])) for i, code in zip(order, coded)
    ]
    home = home_state(
        message,
        suffix_key_value[0],
        suffix_len,
        token_keys[0],
        token_values[0],
        low,
        high,
        near,
        after=coded,
    )
    result = final_output(home, received)
    result = result.reshape(KEY_VALUE_HEADS, -1, steps, HEAD_SIZE)
    return result.transpose(2, 0, 1, 3).reshape(queries.shape)


def solution(mesh):
    sessions = ("ctx", "tab")
    placed = (
        P(sessions, None, None),
        P("ctx", None, None),
        P("tab", "ctx", None, None),
        P(),
        P(sessions),
        P(sessions, None, None, None),
        P(sessions),
        P(sessions, None, None),
        P(sessions, None, None),
    )
    return jax.shard_map(
        shards, mesh=mesh, in_specs=placed, out_specs=P(sessions, None, None), check_vma=False
    )
```

```python
import functools

import jax
import jax.numpy as jnp
from jax import lax
from jax.experimental import pallas as pl
from jax.experimental.pallas import tpu as pltpu
from jax.sharding import PartitionSpec as P

KEY_VALUE_HEADS = 8
HEAD_SIZE = 128
SCALE = HEAD_SIZE**-0.5
SCALE_TWO = SCALE * 1.4426950408889634
MIB = 1024 * 1024
FILLER = -1e30
CODE_TOP = 32000.0
REST_TOP = 65000.0

NT = (((1,), (1,)), ((), ()))


def head_lanes(h):
    return pl.ds(h * HEAD_SIZE, HEAD_SIZE)


def put_lane(slab, lane, column):
    at = lax.broadcasted_iota(jnp.int32, slab.shape, 1)
    return jnp.where(at == lane, column, slab)


def vmem_limit(members, slots=4):
    return (8 if members * slots <= 32 else 48) * MIB


def in_any(count):
    return [pl.BlockSpec(memory_space=pl.ANY)] * count


def in_hbm(count):
    return [pl.BlockSpec(memory_space=pltpu.HBM)] * count


def in_vmem(count):
    return [pl.BlockSpec(memory_space=pltpu.VMEM)] * count


def in_smem(count):
    return [pl.BlockSpec(memory_space=pltpu.SMEM)] * count


def tile_rows(paired):
    tiles = paired.reshape(paired.shape[0], 2, KEY_VALUE_HEADS, HEAD_SIZE)
    return tiles.transpose(0, 2, 1, 3).reshape(-1, HEAD_SIZE)


PER_ROW = 2 * KEY_VALUE_HEADS
EXTRA = 8


def split_rows(tiles, wide, first, count, key_ref, value_ref):
    start = first * PER_ROW
    wide[pl.ds(start, count * PER_ROW)] = tiles[pl.ds(start, count * PER_ROW)].astype(jnp.float32)
    for h in range(KEY_VALUE_HEADS):
        for k, ref in enumerate((key_ref, value_ref)):
            rows = wide[pl.ds(start + 2 * h + k, count, stride=PER_ROW), :]
            ref[pl.ds(first, count), head_lanes(h)] = rows.astype(ref.dtype)


def prepare_kernel(
    session, owner_hbm, query_hbm, tab_hbm, message_ref, block_ref, tiles, wide, owner, sems
):
    moves = [
        (tab_hbm, tiles),
        (owner_hbm, owner),
        (query_hbm, message_ref.at[0, pl.ds(0, query_hbm.shape[0])]),
    ]
    copies = [pltpu.make_async_copy(*move, sems.at[i]) for i, move in enumerate(moves)]
    for copy in copies:
        copy.start()
    copies[1].wait()
    slot = jnp.int32(0)
    for k in range(owner.shape[0]):
        slot = jnp.where(session[0] == k, owner[k], slot)
    filled = jnp.full((EXTRA, HEAD_SIZE), slot.astype(jnp.float32), jnp.float32)
    message_ref[0, pl.ds(query_hbm.shape[0], EXTRA)] = filled.astype(jnp.bfloat16)
    copies[0].wait()
    split_rows(tiles, wide, 0, block_ref.shape[1], block_ref.at[0], block_ref.at[1])
    copies[2].wait()


def stay(arrays):
    return [pltpu.with_memory_space_constraint(array, pltpu.HBM) for array in arrays]


def prepare(session_tab, tab_owner, query, tab):
    tiles = tile_rows(tab)
    return pl.pallas_call(
        prepare_kernel,
        in_specs=in_smem(1) + in_hbm(3),
        out_specs=in_vmem(2),
        out_shape=[
            jax.ShapeDtypeStruct((1, query.shape[0] + EXTRA, HEAD_SIZE), jnp.bfloat16),
            jax.ShapeDtypeStruct((2, tab.shape[0], tab.shape[2]), jnp.bfloat16),
        ],
        scratch_shapes=[
            pltpu.VMEM(tiles.shape, tiles.dtype),
            pltpu.VMEM(tiles.shape, jnp.float32),
            pltpu.SMEM(tab_owner.shape, tab_owner.dtype),
            pltpu.SemaphoreType.DMA((4,)),
        ],
        compiler_params=pltpu.CompilerParams(vmem_limit_bytes=6 * MIB),
        name="prepare",
    )(session_tab, *stay([tab_owner, query, tiles]))


def split_kernel(first, chunks, tiles_hbm, key_ref, value_ref, tiles, wide, sems):
    rows = key_ref.shape[0] // chunks
    piece = rows * PER_ROW
    copies = [
        pltpu.make_async_copy(
            tiles_hbm.at[pl.ds(first * PER_ROW + i * piece, piece)],
            tiles.at[pl.ds(i * piece, piece)],
            sems.at[i],
        )
        for i in range(chunks)
    ]
    for copy in copies:
        copy.start()
    for i, copy in enumerate(copies):
        copy.wait()
        split_rows(tiles, wide, i * rows, rows, key_ref, value_ref)


def split_pairs(tiles, first, rows, chunks=4):
    shape = jax.ShapeDtypeStruct((rows, KEY_VALUE_HEADS * HEAD_SIZE), tiles.dtype)
    scratch = (rows * PER_ROW, HEAD_SIZE)
    return pl.pallas_call(
        functools.partial(split_kernel, first, chunks),
        in_specs=in_hbm(1),
        out_specs=in_vmem(2),
        out_shape=[shape, shape],
        scratch_shapes=[
            pltpu.VMEM(scratch, tiles.dtype),
            pltpu.VMEM(scratch, jnp.float32),
            pltpu.SemaphoreType.DMA((chunks,)),
        ],
        compiler_params=pltpu.CompilerParams(vmem_limit_bytes=6 * MIB),
        name="split_pairs",
    )(*stay([tiles]))


def block_softmax(score_parts, value_parts):
    largest = functools.reduce(
        jnp.maximum, [jnp.max(s, axis=-1, keepdims=True) for s in score_parts]
    )
    product = 0.0
    for scores, values in zip(score_parts, value_parts):
        weights = jnp.exp2((scores - largest) * SCALE_TWO).astype(jnp.bfloat16)
        values = jnp.concatenate([values, jnp.ones_like(values)], axis=1)
        product += jnp.dot(weights, values, preferred_element_type=jnp.float32)
    summed, total = product[:, :HEAD_SIZE], product[:, HEAD_SIZE:]
    return summed / total, largest * SCALE + jnp.log(total)


def row_count(message):
    return (message.shape[-2] - EXTRA) // KEY_VALUE_HEADS


def rows_of(ref, h):
    rows = row_count(ref)
    return ref[pl.ds(h * rows, rows)]


def extra_of(ref):
    return ref[pl.ds(ref.shape[0] - EXTRA, EXTRA)]


def context_kernel(heads, sizes, pieces, shares, slots, column_slot_ref, *refs):
    query_refs = [r.at[i] for r in refs[:pieces] for i in range(r.shape[0])]
    refs = refs[pieces:]
    key_refs, value_refs, refs = refs[:shares], refs[shares : 2 * shares], refs[2 * shares :]
    tab_refs, out_refs, members = refs[:slots], refs[slots:], len(query_refs)
    places = [r.at[i] for r, size in zip(out_refs, sizes) for i in range(size)]
    rows = row_count(query_refs[0])
    owner = jnp.concatenate([extra_of(q)[:, 0:1] for q in query_refs for _ in range(rows // EXTRA)])
    mine = owner.astype(jnp.float32) == column_slot_ref[0:1, :]
    ends = jnp.zeros((members * rows, HEAD_SIZE), jnp.float32)
    for n, h in enumerate(heads):
        at = head_lanes(h)
        query = jnp.concatenate([rows_of(q, h) for q in query_refs], axis=0)
        tab_keys = jnp.concatenate([t[0, :, at] for t in tab_refs], axis=0)
        tab_values = jnp.concatenate([t[1, :, at] for t in tab_refs], axis=0)
        scores = [
            lax.dot_general(query, keys, NT, preferred_element_type=jnp.float32)
            for keys in [r[:, at] for r in key_refs] + [tab_keys]
        ]
        scores[-1] = jnp.where(mine, scores[-1], FILLER)
        mean, end = block_softmax(scores, [r[:, at] for r in value_refs] + [tab_values])
        for i, place in enumerate(places):
            place[n] = mean[i * rows : (i + 1) * rows]
        ends = put_lane(ends, h, end)
    for i, place in enumerate(places):
        place[len(heads)] = ends[i * rows : (i + 1) * rows]


def context_states(heads, sizes, pieces, keys, values, column_slot, tabs):
    members, rows = sum(sizes), row_count(pieces[0])
    key_count = sum(k.shape[0] for k in keys) + column_slot.shape[1]
    work = members * rows * len(heads) * key_count
    return pl.pallas_call(
        functools.partial(context_kernel, heads, sizes, len(pieces), len(keys), len(tabs)),
        in_specs=in_vmem(1 + len(pieces) + 2 * len(keys) + len(tabs)),
        out_specs=in_vmem(len(sizes)),
        out_shape=[
            jax.ShapeDtypeStruct((size, len(heads) + 1, rows, HEAD_SIZE), jnp.float32)
            for size in sizes
        ],
        compiler_params=pltpu.CompilerParams(vmem_limit_bytes=vmem_limit(members, len(tabs))),
        cost_estimate=pl.CostEstimate(
            flops=4 * work * HEAD_SIZE, transcendentals=work, bytes_accessed=1
        ),
        name="context_states",
    )(column_slot, *pieces, *keys, *values, *tabs)


def shares_of(ends):
    top = functools.reduce(jnp.maximum, ends)
    shares = [jnp.exp(end - top) for end in ends]
    total = functools.reduce(jnp.add, shares)
    return [share / total for share in shares], top + jnp.log(total)


def mixed(parts, shares, h):
    return functools.reduce(
        jnp.add, [part * share[:, h : h + 1] for part, share in zip(parts, shares)]
    )


def both_halves(i, low_ref, high_ref):
    halves = [r.at[i, h] for r in (low_ref, high_ref) for h in range(r.shape[1] - 1)]
    return halves, low_ref[i, low_ref.shape[1] - 1] + high_ref[i, high_ref.shape[1] - 1]


def home_kernel(
    steps, length_ref, query_ref, tiles, new_key_ref, new_value_ref, low_ref, high_ref, other_ref, *refs
):
    out_ref, wide, key_ref, value_ref = refs[-4:]
    rows, slots = row_count(query_ref), key_ref.shape[0]
    split_rows(tiles, wide, 0, slots, key_ref, value_ref)
    used = lax.broadcasted_iota(jnp.int32, (rows, slots), 1) < length_ref[0]
    step = lax.rem(lax.broadcasted_iota(jnp.int32, (rows, steps), 0), steps)
    seen = lax.broadcasted_iota(jnp.int32, (rows, steps), 1) <= step
    ends, means = jnp.zeros((rows, HEAD_SIZE), jnp.float32), []
    for h in range(KEY_VALUE_HEADS):
        at = head_lanes(h)
        query = rows_of(query_ref.at[0], h)
        cached = lax.dot_general(query, key_ref[:, at], NT, preferred_element_type=jnp.float32)
        fresh = lax.dot_general(query, new_key_ref[:, at], NT, preferred_element_type=jnp.float32)
        cached = jnp.where(used, cached, FILLER)
        fresh = jnp.where(seen, fresh, FILLER)
        mean, end = block_softmax([cached, fresh], [value_ref[:, at], new_value_ref[:, at]])
        means.append(mean)
        ends = put_lane(ends, h, end)
    own, own_end = both_halves(0, low_ref, high_ref)
    shares, end = shares_of([ends, own_end, other_ref[0, KEY_VALUE_HEADS]])
    for h, mean in enumerate(means):
        out_ref[h] = mixed([mean, own[h][...], other_ref[0, h]], shares, h)
    out_ref[KEY_VALUE_HEADS] = end


def home_state(query_message, cache, length, new_keys, new_values, low, high, other, after):
    rows, steps = row_count(query_message), new_keys.shape[0]
    work = rows * KEY_VALUE_HEADS * cache.shape[0]
    tiles = tile_rows(cache)
    return pl.pallas_call(
        functools.partial(home_kernel, steps),
        in_specs=in_smem(1) + in_vmem(7) + in_any(len(after)),
        out_shape=jax.ShapeDtypeStruct((KEY_VALUE_HEADS + 1, rows, HEAD_SIZE), jnp.float32),
        scratch_shapes=[
            pltpu.VMEM(tiles.shape, jnp.float32),
            pltpu.VMEM((cache.shape[0], cache.shape[2]), cache.dtype),
            pltpu.VMEM((cache.shape[0], cache.shape[2]), cache.dtype),
        ],
        compiler_params=pltpu.CompilerParams(vmem_limit_bytes=vmem_limit(low.shape[0])),
        cost_estimate=pl.CostEstimate(
            flops=4 * work * HEAD_SIZE, transcendentals=work, bytes_accessed=4 * cache.size
        ),
        name="home_state",
    )(length, query_message, tiles, new_keys, new_values, low, high, other, *after)


def pair_kernel(order, low_ref, high_ref, other_ref, *coded_refs):
    rows = other_ref.shape[2]
    for i, coded_ref in zip(order, coded_refs):
        own, own_end = both_halves(i, low_ref, high_ref)
        shares, end = shares_of([own_end, other_ref[i - 1, KEY_VALUE_HEADS]])
        means = [
            mixed([own[h][...], other_ref[i - 1, h]], shares, h) for h in range(KEY_VALUE_HEADS)
        ]
        reach = jnp.ones((rows, HEAD_SIZE), jnp.float32)
        for h, mean in enumerate(means):
            reach = put_lane(reach, h, jnp.max(jnp.abs(mean), axis=-1, keepdims=True))
        exponent = jnp.ceil(jnp.log2(jnp.maximum(reach, 1e-30)))
        factor = jnp.exp2(-exponent) * CODE_TOP
        for h, mean in enumerate(means):
            code = jnp.round(mean * factor[:, h : h + 1])
            coded_ref[pl.ds(h * rows, rows)] = code.astype(jnp.int32).astype(jnp.int16)
        near = jnp.round(end)
        rest = jnp.round((end - near) * REST_TOP)
        at = lax.broadcasted_iota(jnp.int32, (EXTRA, HEAD_SIZE), 1) // KEY_VALUE_HEADS
        slab, kinds = jnp.zeros((EXTRA, HEAD_SIZE), jnp.float32), (near, rest, exponent)
        for r in range(rows // EXTRA):
            for k, kind in enumerate(kinds):
                place = r * len(kinds) + k
                part = kind[r * EXTRA : (r + 1) * EXTRA]
                moved = pltpu.roll(part, place * KEY_VALUE_HEADS, 1) if place else part
                slab = jnp.where(at == place, moved, slab)
        coded_ref[pl.ds(KEY_VALUE_HEADS * rows, EXTRA)] = slab.astype(jnp.int32).astype(jnp.int16)


def pair_states(order, low, high, other):
    rows = other.shape[2]
    shape = (KEY_VALUE_HEADS * rows + EXTRA, HEAD_SIZE)
    return pl.pallas_call(
        functools.partial(pair_kernel, order),
        out_shape=[jax.ShapeDtypeStruct(shape, jnp.int16)] * len(order),
        compiler_params=pltpu.CompilerParams(vmem_limit_bytes=vmem_limit(low.shape[0])),
        name="pair_states",
    )(low, high, other)


def final_kernel(home_ref, *refs):
    coded_refs, out_ref = refs[:-1], refs[-1]
    rows = home_ref.shape[1]
    ends, factors = [home_ref[KEY_VALUE_HEADS]], []
    head_lane = lax.broadcasted_iota(jnp.int32, ends[0].shape, 1) < KEY_VALUE_HEADS
    for r in coded_refs:
        slab = extra_of(r).astype(jnp.int32).astype(jnp.float32)
        near, rest, exponent = (
            jnp.concatenate(
                [
                    pltpu.roll(slab, (HEAD_SIZE - (3 * i + k) * KEY_VALUE_HEADS) % HEAD_SIZE, 1)
                    for i in range(rows // EXTRA)
                ]
            )
            for k in range(3)
        )
        ends.append(near + rest / REST_TOP)
        factors.append(jnp.exp2(jnp.where(head_lane, exponent, 0.0)) / CODE_TOP)
    shares, _ = shares_of([jnp.where(head_lane, end, 0.0) for end in ends])
    shares = shares[:1] + [share * factor for share, factor in zip(shares[1:], factors)]
    for h in range(KEY_VALUE_HEADS):
        parts = [rows_of(r, h).astype(jnp.int32).astype(jnp.float32) for r in coded_refs]
        out_ref[h] = mixed([home_ref[h]] + parts, shares, h).astype(jnp.bfloat16)


def final_output(home, coded):
    return pl.pallas_call(
        final_kernel,
        out_shape=jax.ShapeDtypeStruct((KEY_VALUE_HEADS,) + home.shape[1:], jnp.bfloat16),
        compiler_params=pltpu.CompilerParams(vmem_limit_bytes=vmem_limit(len(coded))),
        name="final_output",
    )(home, *coded)


def swap(count, bit):
    return [(i, i ^ bit) for i in range(count)]


def shards(
    queries,
    prefix_key_value,
    tab_key_value,
    tab_owner,
    session_tab,
    suffix_key_value,
    suffix_len,
    token_keys,
    token_values,
):
    ctx_count, tab_count = lax.axis_size("ctx"), lax.axis_size("tab")
    pair_count = ctx_count // 2
    steps = queries.shape[1]
    tab_rows = tab_key_value.shape[1]

    query = queries[0].reshape(steps, KEY_VALUE_HEADS, -1, HEAD_SIZE)
    query = query.transpose(1, 2, 0, 3).reshape(-1, HEAD_SIZE)
    message, tab_block = prepare(session_tab, tab_owner, query, tab_key_value[0])
    tabs = [tab_block] + [
        lax.ppermute(tab_block, "tab", swap(tab_count, k)) for k in range(1, tab_count)
    ]
    places = jnp.arange(tab_count * tab_rows, dtype=jnp.int32) // tab_rows
    column_slot = (places ^ lax.axis_index("tab")).astype(jnp.float32)[None]

    tiles = tile_rows(prefix_key_value)
    half = prefix_key_value.shape[0] // 2
    splits = [split_pairs(tiles, i * half, half) for i in range(2)]
    pieces, masks, bit = [message], [0], pair_count // 2
    while bit:
        if len(masks) == 2:
            pieces[-1], splits[0] = lax.optimization_barrier((pieces[-1], splits[0]))
        column = jnp.concatenate(pieces, axis=0) if len(pieces) > 1 else message
        pieces = [column, lax.ppermute(column, "ctx", swap(ctx_count, 2 * bit))]
        masks, bit = masks + [mask ^ bit for mask in masks], bit // 2
    pieces[-1], tabs, splits = lax.optimization_barrier((pieces[-1], tabs, splits))
    other_pieces = [lax.ppermute(piece, "ctx", swap(ctx_count, 1)) for piece in pieces]
    keys, values = zip(*splits)
    shared = (keys, values, column_slot, tabs)
    heads = tuple(range(KEY_VALUE_HEADS))
    first, second = heads[:5], heads[5:]
    (low,) = context_states(first, (pair_count,), pieces, *shared)
    other_pieces, low = lax.optimization_barrier((other_pieces, low))
    near, far = context_states(heads, (1, pair_count - 1), other_pieces, *shared)
    pieces, far = lax.optimization_barrier((pieces, far))
    far = lax.ppermute(far, "ctx", swap(ctx_count, 1))
    near = lax.ppermute(near, "ctx", swap(ctx_count, 1))
    (high,) = context_states(second, (pair_count,), pieces, *shared)
    order = sorted(range(1, pair_count), key=lambda i: (masks[i] < pair_count // 2, masks[i]))
    coded = pair_states(order, low, high, far)
    received = [
        lax.ppermute(code, "ctx", swap(ctx_count, 2 * masks[i])) for i, code in zip(order, coded)
    ]
    home = home_state(
        message,
        suffix_key_value[0],
        suffix_len,
        token_keys[0],
        token_values[0],
        low,
        high,
        near,
        after=coded,
    )
    result = final_output(home, received)
    result = result.reshape(KEY_VALUE_HEADS, -1, steps, HEAD_SIZE)
    return result.transpose(2, 0, 1, 3).reshape(queries.shape)


def solution(mesh):
    sessions = ("ctx", "tab")
    placed = (
        P(sessions, None, None),
        P("ctx", None, None),
        P("tab", "ctx", None, None),
        P(),
        P(sessions),
        P(sessions, None, None, None),
        P(sessions),
        P(sessions, None, None),
        P(sessions, None, None),
    )
    return jax.shard_map(
        shards, mesh=mesh, in_specs=placed, out_specs=P(sessions, None, None), check_vma=False
    )
```

```python
import functools

import jax
import jax.numpy as jnp
from jax import lax
from jax.experimental import pallas as pl
from jax.experimental.pallas import tpu as pltpu
from jax.sharding import PartitionSpec as P

KEY_VALUE_HEADS = 8
HEAD_SIZE = 128
SCALE = HEAD_SIZE**-0.5
SCALE_TWO = SCALE * 1.4426950408889634
MIB = 1024 * 1024
FILLER = -1e30
CODE_TOP = 32000.0
REST_TOP = 65000.0

NT = (((1,), (1,)), ((), ()))


def head_lanes(h):
    return pl.ds(h * HEAD_SIZE, HEAD_SIZE)


def put_lane(slab, lane, column):
    at = lax.broadcasted_iota(jnp.int32, slab.shape, 1)
    return jnp.where(at == lane, column, slab)


def vmem_limit(members, slots=4):
    return (8 if members * slots <= 32 else 48) * MIB


def in_any(count):
    return [pl.BlockSpec(memory_space=pl.ANY)] * count


def in_hbm(count):
    return [pl.BlockSpec(memory_space=pltpu.HBM)] * count


def in_vmem(count):
    return [pl.BlockSpec(memory_space=pltpu.VMEM)] * count


def in_smem(count):
    return [pl.BlockSpec(memory_space=pltpu.SMEM)] * count


def tile_rows(paired):
    tiles = paired.reshape(paired.shape[0], 2, KEY_VALUE_HEADS, HEAD_SIZE)
    return tiles.transpose(0, 2, 1, 3).reshape(-1, HEAD_SIZE)


PER_ROW = 2 * KEY_VALUE_HEADS
EXTRA = 8


def split_rows(tiles, wide, first, count, key_ref, value_ref):
    start = first * PER_ROW
    wide[pl.ds(start, count * PER_ROW)] = tiles[pl.ds(start, count * PER_ROW)].astype(jnp.float32)
    for h in range(KEY_VALUE_HEADS):
        for k, ref in enumerate((key_ref, value_ref)):
            rows = wide[pl.ds(start + 2 * h + k, count, stride=PER_ROW), :]
            ref[pl.ds(first, count), head_lanes(h)] = rows.astype(ref.dtype)


def prepare_kernel(
    session, owner_hbm, query_hbm, tab_hbm, message_ref, block_ref, tiles, wide, owner, sems
):
    moves = [
        (tab_hbm, tiles),
        (owner_hbm, owner),
        (query_hbm, message_ref.at[0, pl.ds(0, query_hbm.shape[0])]),
    ]
    copies = [pltpu.make_async_copy(*move, sems.at[i]) for i, move in enumerate(moves)]
    for copy in copies:
        copy.start()
    copies[1].wait()
    slot = jnp.int32(0)
    for k in range(owner.shape[0]):
        slot = jnp.where(session[0] == k, owner[k], slot)
    filled = jnp.full((EXTRA, HEAD_SIZE), slot.astype(jnp.float32), jnp.float32)
    message_ref[0, pl.ds(query_hbm.shape[0], EXTRA)] = filled.astype(jnp.bfloat16)
    copies[0].wait()
    split_rows(tiles, wide, 0, block_ref.shape[1], block_ref.at[0], block_ref.at[1])
    copies[2].wait()


def stay(arrays):
    return [pltpu.with_memory_space_constraint(array, pltpu.HBM) for array in arrays]


def prepare(session_tab, tab_owner, query, tab):
    tiles = tile_rows(tab)
    return pl.pallas_call(
        prepare_kernel,
        in_specs=in_smem(1) + in_hbm(3),
        out_specs=in_vmem(2),
        out_shape=[
            jax.ShapeDtypeStruct((1, query.shape[0] + EXTRA, HEAD_SIZE), jnp.bfloat16),
            jax.ShapeDtypeStruct((2, tab.shape[0], tab.shape[2]), jnp.bfloat16),
        ],
        scratch_shapes=[
            pltpu.VMEM(tiles.shape, tiles.dtype),
            pltpu.VMEM(tiles.shape, jnp.float32),
            pltpu.SMEM(tab_owner.shape, tab_owner.dtype),
            pltpu.SemaphoreType.DMA((4,)),
        ],
        compiler_params=pltpu.CompilerParams(vmem_limit_bytes=6 * MIB),
        name="prepare",
    )(session_tab, *stay([tab_owner, query, tiles]))


def split_kernel(first, chunks, tiles_hbm, key_ref, value_ref, tiles, wide, sems):
    rows = key_ref.shape[0] // chunks
    piece = rows * PER_ROW
    copies = [
        pltpu.make_async_copy(
            tiles_hbm.at[pl.ds(first * PER_ROW + i * piece, piece)],
            tiles.at[pl.ds(i * piece, piece)],
            sems.at[i],
        )
        for i in range(chunks)
    ]
    for copy in copies:
        copy.start()
    for i, copy in enumerate(copies):
        copy.wait()
        split_rows(tiles, wide, i * rows, rows, key_ref, value_ref)


def split_pairs(tiles, first, rows, chunks=4):
    shape = jax.ShapeDtypeStruct((rows, KEY_VALUE_HEADS * HEAD_SIZE), tiles.dtype)
    scratch = (rows * PER_ROW, HEAD_SIZE)
    return pl.pallas_call(
        functools.partial(split_kernel, first, chunks),
        in_specs=in_hbm(1),
        out_specs=in_vmem(2),
        out_shape=[shape, shape],
        scratch_shapes=[
            pltpu.VMEM(scratch, tiles.dtype),
            pltpu.VMEM(scratch, jnp.float32),
            pltpu.SemaphoreType.DMA((chunks,)),
        ],
        compiler_params=pltpu.CompilerParams(vmem_limit_bytes=6 * MIB),
        name="split_pairs",
    )(*stay([tiles]))


def block_softmax(score_parts, value_parts):
    largest = functools.reduce(
        jnp.maximum, [jnp.max(s, axis=-1, keepdims=True) for s in score_parts]
    )
    product = 0.0
    for scores, values in zip(score_parts, value_parts):
        weights = jnp.exp2((scores - largest) * SCALE_TWO).astype(jnp.bfloat16)
        values = jnp.concatenate([values, jnp.ones_like(values)], axis=1)
        product += jnp.dot(weights, values, preferred_element_type=jnp.float32)
    summed, total = product[:, :HEAD_SIZE], product[:, HEAD_SIZE:]
    return summed / total, largest * SCALE + jnp.log(total)


def row_count(message):
    return (message.shape[-2] - EXTRA) // KEY_VALUE_HEADS


def rows_of(ref, h):
    rows = row_count(ref)
    return ref[pl.ds(h * rows, rows)]


def extra_of(ref):
    return ref[pl.ds(ref.shape[0] - EXTRA, EXTRA)]


def context_kernel(heads, groups, pieces, shares, slots, column_slot_ref, *refs):
    query_refs = [r.at[i] for r in refs[:pieces] for i in range(r.shape[0])]
    refs = refs[pieces:]
    key_refs, value_refs, refs = refs[:shares], refs[shares : 2 * shares], refs[2 * shares :]
    tab_refs, out_refs, members = refs[:slots], refs[slots:], len(query_refs)
    places = [(i, r.at[n]) for r, group in zip(out_refs, groups) for n, i in enumerate(group)]
    rows = row_count(query_refs[0])
    owner = jnp.concatenate([extra_of(q)[:, 0:1] for q in query_refs for _ in range(rows // EXTRA)])
    mine = owner.astype(jnp.float32) == column_slot_ref[0:1, :]
    ends = jnp.zeros((members * rows, HEAD_SIZE), jnp.float32)
    for n, h in enumerate(heads):
        at = head_lanes(h)
        query = jnp.concatenate([rows_of(q, h) for q in query_refs], axis=0)
        tab_keys = jnp.concatenate([t[0, :, at] for t in tab_refs], axis=0)
        tab_values = jnp.concatenate([t[1, :, at] for t in tab_refs], axis=0)
        scores = [
            lax.dot_general(query, keys, NT, preferred_element_type=jnp.float32)
            for keys in [r[:, at] for r in key_refs] + [tab_keys]
        ]
        scores[-1] = jnp.where(mine, scores[-1], FILLER)
        mean, end = block_softmax(scores, [r[:, at] for r in value_refs] + [tab_values])
        for i, place in places:
            place[n] = mean[i * rows : (i + 1) * rows]
        ends = put_lane(ends, h, end)
    for i, place in places:
        place[len(heads)] = ends[i * rows : (i + 1) * rows]


def context_states(heads, groups, pieces, keys, values, column_slot, tabs):
    members, rows = sum(len(group) for group in groups), row_count(pieces[0])
    key_count = sum(k.shape[0] for k in keys) + column_slot.shape[1]
    work = members * rows * len(heads) * key_count
    return pl.pallas_call(
        functools.partial(context_kernel, heads, groups, len(pieces), len(keys), len(tabs)),
        in_specs=in_vmem(1 + len(pieces) + 2 * len(keys) + len(tabs)),
        out_specs=in_vmem(len(groups)),
        out_shape=[
            jax.ShapeDtypeStruct((len(group), len(heads) + 1, rows, HEAD_SIZE), jnp.float32)
            for group in groups
        ],
        compiler_params=pltpu.CompilerParams(vmem_limit_bytes=vmem_limit(members, len(tabs))),
        cost_estimate=pl.CostEstimate(
            flops=4 * work * HEAD_SIZE, transcendentals=work, bytes_accessed=1
        ),
        name="context_states",
    )(column_slot, *pieces, *keys, *values, *tabs)


def shares_of(ends):
    top = functools.reduce(jnp.maximum, ends)
    shares = [jnp.exp(end - top) for end in ends]
    total = functools.reduce(jnp.add, shares)
    return [share / total for share in shares], top + jnp.log(total)


def mixed(parts, shares, h):
    return functools.reduce(
        jnp.add, [part * share[:, h : h + 1] for part, share in zip(parts, shares)]
    )


def both_halves(i, low_ref, high_ref):
    halves = [r.at[i, h] for r in (low_ref, high_ref) for h in range(r.shape[1] - 1)]
    return halves, low_ref[i, low_ref.shape[1] - 1] + high_ref[i, high_ref.shape[1] - 1]


def home_kernel(
    steps, length_ref, query_ref, tiles, new_key_ref, new_value_ref, low_ref, high_ref, other_ref, *refs
):
    out_ref, wide, key_ref, value_ref = refs[-4:]
    rows, slots = row_count(query_ref), key_ref.shape[0]
    split_rows(tiles, wide, 0, slots, key_ref, value_ref)
    used = lax.broadcasted_iota(jnp.int32, (rows, slots), 1) < length_ref[0]
    step = lax.rem(lax.broadcasted_iota(jnp.int32, (rows, steps), 0), steps)
    seen = lax.broadcasted_iota(jnp.int32, (rows, steps), 1) <= step
    ends, means = jnp.zeros((rows, HEAD_SIZE), jnp.float32), []
    for h in range(KEY_VALUE_HEADS):
        at = head_lanes(h)
        query = rows_of(query_ref.at[0], h)
        cached = lax.dot_general(query, key_ref[:, at], NT, preferred_element_type=jnp.float32)
        fresh = lax.dot_general(query, new_key_ref[:, at], NT, preferred_element_type=jnp.float32)
        cached = jnp.where(used, cached, FILLER)
        fresh = jnp.where(seen, fresh, FILLER)
        mean, end = block_softmax([cached, fresh], [value_ref[:, at], new_value_ref[:, at]])
        means.append(mean)
        ends = put_lane(ends, h, end)
    own, own_end = both_halves(0, low_ref, high_ref)
    shares, end = shares_of([ends, own_end, other_ref[0, KEY_VALUE_HEADS]])
    for h, mean in enumerate(means):
        out_ref[h] = mixed([mean, own[h][...], other_ref[0, h]], shares, h)
    out_ref[KEY_VALUE_HEADS] = end


def home_state(query_message, cache, length, new_keys, new_values, low, high, other, after):
    rows, steps = row_count(query_message), new_keys.shape[0]
    work = rows * KEY_VALUE_HEADS * cache.shape[0]
    tiles = tile_rows(cache)
    return pl.pallas_call(
        functools.partial(home_kernel, steps),
        in_specs=in_smem(1) + in_vmem(7) + in_any(len(after)),
        out_shape=jax.ShapeDtypeStruct((KEY_VALUE_HEADS + 1, rows, HEAD_SIZE), jnp.float32),
        scratch_shapes=[
            pltpu.VMEM(tiles.shape, jnp.float32),
            pltpu.VMEM((cache.shape[0], cache.shape[2]), cache.dtype),
            pltpu.VMEM((cache.shape[0], cache.shape[2]), cache.dtype),
        ],
        compiler_params=pltpu.CompilerParams(vmem_limit_bytes=vmem_limit(low.shape[0])),
        cost_estimate=pl.CostEstimate(
            flops=4 * work * HEAD_SIZE, transcendentals=work, bytes_accessed=4 * cache.size
        ),
        name="home_state",
    )(length, query_message, tiles, new_keys, new_values, low, high, other, *after)


def pair_kernel(order, low_ref, high_ref, other_ref, *coded_refs):
    rows = other_ref.shape[2]
    for (i, at), coded_ref in zip(order, coded_refs):
        own, own_end = both_halves(i, low_ref, high_ref)
        shares, end = shares_of([own_end, other_ref[at, KEY_VALUE_HEADS]])
        means = [
            mixed([own[h][...], other_ref[at, h]], shares, h) for h in range(KEY_VALUE_HEADS)
        ]
        reach = jnp.ones((rows, HEAD_SIZE), jnp.float32)
        for h, mean in enumerate(means):
            reach = put_lane(reach, h, jnp.max(jnp.abs(mean), axis=-1, keepdims=True))
        exponent = jnp.ceil(jnp.log2(jnp.maximum(reach, 1e-30)))
        factor = jnp.exp2(-exponent) * CODE_TOP
        for h, mean in enumerate(means):
            code = jnp.round(mean * factor[:, h : h + 1])
            coded_ref[pl.ds(h * rows, rows)] = code.astype(jnp.int32).astype(jnp.int16)
        near = jnp.round(end)
        rest = jnp.round((end - near) * REST_TOP)
        lane = lax.broadcasted_iota(jnp.int32, (EXTRA, HEAD_SIZE), 1) // KEY_VALUE_HEADS
        slab, kinds = jnp.zeros((EXTRA, HEAD_SIZE), jnp.float32), (near, rest, exponent)
        for r in range(rows // EXTRA):
            for k, kind in enumerate(kinds):
                place = r * len(kinds) + k
                part = kind[r * EXTRA : (r + 1) * EXTRA]
                moved = pltpu.roll(part, place * KEY_VALUE_HEADS, 1) if place else part
                slab = jnp.where(lane == place, moved, slab)
        coded_ref[pl.ds(KEY_VALUE_HEADS * rows, EXTRA)] = slab.astype(jnp.int32).astype(jnp.int16)


def pair_states(order, low, high, other):
    rows = other.shape[2]
    shape = (KEY_VALUE_HEADS * rows + EXTRA, HEAD_SIZE)
    return pl.pallas_call(
        functools.partial(pair_kernel, order),
        out_shape=[jax.ShapeDtypeStruct(shape, jnp.int16)] * len(order),
        compiler_params=pltpu.CompilerParams(vmem_limit_bytes=vmem_limit(low.shape[0])),
        name="pair_states",
    )(low, high, other)


def final_kernel(home_ref, *refs):
    coded_refs, out_ref = refs[:-1], refs[-1]
    rows = home_ref.shape[1]
    ends, factors = [home_ref[KEY_VALUE_HEADS]], []
    head_lane = lax.broadcasted_iota(jnp.int32, ends[0].shape, 1) < KEY_VALUE_HEADS
    for r in coded_refs:
        slab = extra_of(r).astype(jnp.int32).astype(jnp.float32)
        near, rest, exponent = (
            jnp.concatenate(
                [
                    pltpu.roll(slab, (HEAD_SIZE - (3 * i + k) * KEY_VALUE_HEADS) % HEAD_SIZE, 1)
                    for i in range(rows // EXTRA)
                ]
            )
            for k in range(3)
        )
        ends.append(near + rest / REST_TOP)
        factors.append(jnp.exp2(jnp.where(head_lane, exponent, 0.0)) / CODE_TOP)
    shares, _ = shares_of([jnp.where(head_lane, end, 0.0) for end in ends])
    shares = shares[:1] + [share * factor for share, factor in zip(shares[1:], factors)]
    for h in range(KEY_VALUE_HEADS):
        parts = [rows_of(r, h).astype(jnp.int32).astype(jnp.float32) for r in coded_refs]
        out_ref[h] = mixed([home_ref[h]] + parts, shares, h).astype(jnp.bfloat16)


def final_output(home, coded):
    return pl.pallas_call(
        final_kernel,
        out_shape=jax.ShapeDtypeStruct((KEY_VALUE_HEADS,) + home.shape[1:], jnp.bfloat16),
        compiler_params=pltpu.CompilerParams(vmem_limit_bytes=vmem_limit(len(coded))),
        name="final_output",
    )(home, *coded)


def swap(count, bit):
    return [(i, i ^ bit) for i in range(count)]


def shards(
    queries,
    prefix_key_value,
    tab_key_value,
    tab_owner,
    session_tab,
    suffix_key_value,
    suffix_len,
    token_keys,
    token_values,
):
    ctx_count, tab_count = lax.axis_size("ctx"), lax.axis_size("tab")
    pair_count = ctx_count // 2
    steps = queries.shape[1]
    tab_rows = tab_key_value.shape[1]

    query = queries[0].reshape(steps, KEY_VALUE_HEADS, -1, HEAD_SIZE)
    query = query.transpose(1, 2, 0, 3).reshape(-1, HEAD_SIZE)
    message, tab_block = prepare(session_tab, tab_owner, query, tab_key_value[0])
    tabs = [tab_block] + [
        lax.ppermute(tab_block, "tab", swap(tab_count, k)) for k in range(1, tab_count)
    ]
    places = jnp.arange(tab_count * tab_rows, dtype=jnp.int32) // tab_rows
    column_slot = (places ^ lax.axis_index("tab")).astype(jnp.float32)[None]

    tiles = tile_rows(prefix_key_value)
    half = prefix_key_value.shape[0] // 2
    splits = [split_pairs(tiles, i * half, half) for i in range(2)]
    pieces, masks, bit = [message], [0], pair_count // 2
    while bit:
        if len(masks) == 2:
            pieces[-1], splits[0] = lax.optimization_barrier((pieces[-1], splits[0]))
        column = jnp.concatenate(pieces, axis=0) if len(pieces) > 1 else message
        pieces = [column, lax.ppermute(column, "ctx", swap(ctx_count, 2 * bit))]
        masks, bit = masks + [mask ^ bit for mask in masks], bit // 2
    pieces[-1], tabs, splits = lax.optimization_barrier((pieces[-1], tabs, splits))
    other_pieces = [lax.ppermute(piece, "ctx", swap(ctx_count, 1)) for piece in pieces]
    keys, values = zip(*splits)
    shared = (keys, values, column_slot, tabs)
    heads = tuple(range(KEY_VALUE_HEADS))
    first, second = heads[:5], heads[5:]
    members = range(pair_count)
    far = [i for i in members if masks[i] >= pair_count // 2]
    rest = [i for i in members if i not in far]
    (low,) = context_states(first, [members], pieces, *shared)
    other_pieces, low = lax.optimization_barrier((other_pieces, low))
    others = context_states(heads, [far, rest], other_pieces, *shared)
    pieces, others = lax.optimization_barrier((pieces, others))
    others = list(others)
    others[0] = lax.ppermute(others[0], "ctx", swap(ctx_count, 1))
    (high,) = context_states(second, [members], pieces, *shared)
    coded, received = [], []
    for group, other in zip((far, rest), others):
        if coded:
            coded, other = lax.optimization_barrier((coded, other))
            other = others[1] = lax.ppermute(other, "ctx", swap(ctx_count, 1))
        order = [(i, at) for at, i in enumerate(group) if i]
        if order:
            codes = pair_states(order, low, high, other)
            coded += codes
            received += [
                lax.ppermute(code, "ctx", swap(ctx_count, 2 * masks[i]))
                for (i, _), code in zip(order, codes)
            ]
    home = home_state(
        message,
        suffix_key_value[0],
        suffix_len,
        token_keys[0],
        token_values[0],
        low,
        high,
        others[1],
        after=coded,
    )
    result = final_output(home, received)
    result = result.reshape(KEY_VALUE_HEADS, -1, steps, HEAD_SIZE)
    return result.transpose(2, 0, 1, 3).reshape(queries.shape)


def solution(mesh):
    sessions = ("ctx", "tab")
    placed = (
        P(sessions, None, None),
        P("ctx", None, None),
        P("tab", "ctx", None, None),
        P(),
        P(sessions),
        P(sessions, None, None, None),
        P(sessions),
        P(sessions, None, None),
        P(sessions, None, None),
    )
    return jax.shard_map(
        shards, mesh=mesh, in_specs=placed, out_specs=P(sessions, None, None), check_vma=False
    )
```

```python
import functools

import jax
import jax.numpy as jnp
from jax import lax
from jax.experimental import pallas as pl
from jax.experimental.pallas import tpu as pltpu
from jax.sharding import PartitionSpec as P

KEY_VALUE_HEADS = 8
HEAD_SIZE = 128
SCALE = HEAD_SIZE**-0.5
SCALE_TWO = SCALE * 1.4426950408889634
MIB = 1024 * 1024
FILLER = -1e30
CODE_TOP = 32000.0
REST_TOP = 65000.0

NT = (((1,), (1,)), ((), ()))


def head_lanes(h):
    return pl.ds(h * HEAD_SIZE, HEAD_SIZE)


def put_lane(slab, lane, column):
    at = lax.broadcasted_iota(jnp.int32, slab.shape, 1)
    return jnp.where(at == lane, column, slab)


def vmem_limit(members, slots=4):
    return (8 if members * slots <= 32 else 48) * MIB


def in_any(count):
    return [pl.BlockSpec(memory_space=pl.ANY)] * count


def in_hbm(count):
    return [pl.BlockSpec(memory_space=pltpu.HBM)] * count


def in_vmem(count):
    return [pl.BlockSpec(memory_space=pltpu.VMEM)] * count


def in_smem(count):
    return [pl.BlockSpec(memory_space=pltpu.SMEM)] * count


def tile_rows(paired):
    tiles = paired.reshape(paired.shape[0], 2, KEY_VALUE_HEADS, HEAD_SIZE)
    return tiles.transpose(0, 2, 1, 3).reshape(-1, HEAD_SIZE)


PER_ROW = 2 * KEY_VALUE_HEADS
EXTRA = 8


def split_rows(tiles, wide, first, count, key_ref, value_ref):
    start = first * PER_ROW
    wide[pl.ds(start, count * PER_ROW)] = tiles[pl.ds(start, count * PER_ROW)].astype(jnp.float32)
    for h in range(KEY_VALUE_HEADS):
        for k, ref in enumerate((key_ref, value_ref)):
            rows = wide[pl.ds(start + 2 * h + k, count, stride=PER_ROW), :]
            ref[pl.ds(first, count), head_lanes(h)] = rows.astype(ref.dtype)


def prepare_kernel(
    session, owner_hbm, query_hbm, tab_hbm, message_ref, block_ref, tiles, wide, owner, sems
):
    half = tiles.shape[0] // 2
    moves = [
        (tab_hbm.at[pl.ds(0, half)], tiles.at[pl.ds(0, half)]),
        (owner_hbm, owner),
        (tab_hbm.at[pl.ds(half, half)], tiles.at[pl.ds(half, half)]),
        (query_hbm, message_ref.at[0, pl.ds(0, query_hbm.shape[0])]),
    ]
    copies = [pltpu.make_async_copy(*move, sems.at[i]) for i, move in enumerate(moves)]
    for copy in copies:
        copy.start()
    copies[1].wait()
    slot = jnp.int32(0)
    for k in range(owner.shape[0]):
        slot = jnp.where(session[0] == k, owner[k], slot)
    filled = jnp.full((EXTRA, HEAD_SIZE), slot.astype(jnp.float32), jnp.float32)
    message_ref[0, pl.ds(query_hbm.shape[0], EXTRA)] = filled.astype(jnp.bfloat16)
    copies[0].wait()
    rows = block_ref.shape[1] // 2
    split_rows(tiles, wide, 0, rows, block_ref.at[0], block_ref.at[1])
    copies[2].wait()
    split_rows(tiles, wide, rows, rows, block_ref.at[0], block_ref.at[1])
    copies[3].wait()


def stay(arrays):
    return [pltpu.with_memory_space_constraint(array, pltpu.HBM) for array in arrays]


def prepare(session_tab, tab_owner, query, tab):
    tiles = tile_rows(tab)
    return pl.pallas_call(
        prepare_kernel,
        in_specs=in_smem(1) + in_hbm(3),
        out_specs=in_vmem(2),
        out_shape=[
            jax.ShapeDtypeStruct((1, query.shape[0] + EXTRA, HEAD_SIZE), jnp.bfloat16),
            jax.ShapeDtypeStruct((2, tab.shape[0], tab.shape[2]), jnp.bfloat16),
        ],
        scratch_shapes=[
            pltpu.VMEM(tiles.shape, tiles.dtype),
            pltpu.VMEM(tiles.shape, jnp.float32),
            pltpu.SMEM(tab_owner.shape, tab_owner.dtype),
            pltpu.SemaphoreType.DMA((4,)),
        ],
        compiler_params=pltpu.CompilerParams(vmem_limit_bytes=6 * MIB),
        name="prepare",
    )(session_tab, *stay([tab_owner, query, tiles]))


def split_kernel(first, chunks, tiles_hbm, key_ref, value_ref, tiles, wide, sems):
    rows = key_ref.shape[0] // chunks
    piece = rows * PER_ROW
    copies = [
        pltpu.make_async_copy(
            tiles_hbm.at[pl.ds(first * PER_ROW + i * piece, piece)],
            tiles.at[pl.ds(i * piece, piece)],
            sems.at[i],
        )
        for i in range(chunks)
    ]
    for copy in copies:
        copy.start()
    for i, copy in enumerate(copies):
        copy.wait()
        split_rows(tiles, wide, i * rows, rows, key_ref, value_ref)


def split_pairs(tiles, first, rows, chunks=2):
    shape = jax.ShapeDtypeStruct((rows, KEY_VALUE_HEADS * HEAD_SIZE), tiles.dtype)
    scratch = (rows * PER_ROW, HEAD_SIZE)
    return pl.pallas_call(
        functools.partial(split_kernel, first, chunks),
        in_specs=in_hbm(1),
        out_specs=in_vmem(2),
        out_shape=[shape, shape],
        scratch_shapes=[
            pltpu.VMEM(scratch, tiles.dtype),
            pltpu.VMEM(scratch, jnp.float32),
            pltpu.SemaphoreType.DMA((chunks,)),
        ],
        compiler_params=pltpu.CompilerParams(vmem_limit_bytes=6 * MIB),
        name="split_pairs",
    )(*stay([tiles]))


def block_softmax(score_parts, value_parts):
    largest = functools.reduce(
        jnp.maximum, [jnp.max(s, axis=-1, keepdims=True) for s in score_parts]
    )
    product = 0.0
    for scores, values in zip(score_parts, value_parts):
        weights = jnp.exp2((scores - largest) * SCALE_TWO).astype(jnp.bfloat16)
        values = jnp.concatenate([values, jnp.ones_like(values)], axis=1)
        product += jnp.dot(weights, values, preferred_element_type=jnp.float32)
    summed, total = product[:, :HEAD_SIZE], product[:, HEAD_SIZE:]
    return summed / total, largest * SCALE + jnp.log(total)


def row_count(message):
    return (message.shape[-2] - EXTRA) // KEY_VALUE_HEADS


def rows_of(ref, h):
    rows = row_count(ref)
    return ref[pl.ds(h * rows, rows)]


def extra_of(ref):
    return ref[pl.ds(ref.shape[0] - EXTRA, EXTRA)]


def context_kernel(heads, groups, pieces, shares, slots, column_slot_ref, *refs):
    query_refs = [r.at[i] for r in refs[:pieces] for i in range(r.shape[0])]
    refs = refs[pieces:]
    key_refs, value_refs, refs = refs[:shares], refs[shares : 2 * shares], refs[2 * shares :]
    tab_refs, out_refs, members = refs[:slots], refs[slots:], len(query_refs)
    places = [(i, r.at[n]) for r, group in zip(out_refs, groups) for n, i in enumerate(group)]
    rows = row_count(query_refs[0])
    owner = jnp.concatenate([extra_of(q)[:, 0:1] for q in query_refs for _ in range(rows // EXTRA)])
    mine = owner.astype(jnp.float32) == column_slot_ref[0:1, :]
    ends = jnp.zeros((members * rows, HEAD_SIZE), jnp.float32)
    for n, h in enumerate(heads):
        at = head_lanes(h)
        query = jnp.concatenate([rows_of(q, h) for q in query_refs], axis=0)
        tab_keys = jnp.concatenate([t[0, :, at] for t in tab_refs], axis=0)
        tab_values = jnp.concatenate([t[1, :, at] for t in tab_refs], axis=0)
        scores = [
            lax.dot_general(query, keys, NT, preferred_element_type=jnp.float32)
            for keys in [r[:, at] for r in key_refs] + [tab_keys]
        ]
        scores[-1] = jnp.where(mine, scores[-1], FILLER)
        mean, end = block_softmax(scores, [r[:, at] for r in value_refs] + [tab_values])
        for i, place in places:
            place[n] = mean[i * rows : (i + 1) * rows]
        ends = put_lane(ends, h, end)
    for i, place in places:
        place[len(heads)] = ends[i * rows : (i + 1) * rows]


def context_states(heads, groups, pieces, keys, values, column_slot, tabs):
    members, rows = sum(len(group) for group in groups), row_count(pieces[0])
    key_count = sum(k.shape[0] for k in keys) + column_slot.shape[1]
    work = members * rows * len(heads) * key_count
    return pl.pallas_call(
        functools.partial(context_kernel, heads, groups, len(pieces), len(keys), len(tabs)),
        in_specs=in_vmem(1 + len(pieces) + 2 * len(keys) + len(tabs)),
        out_specs=in_vmem(len(groups)),
        out_shape=[
            jax.ShapeDtypeStruct((len(group), len(heads) + 1, rows, HEAD_SIZE), jnp.float32)
            for group in groups
        ],
        compiler_params=pltpu.CompilerParams(vmem_limit_bytes=vmem_limit(members, len(tabs))),
        cost_estimate=pl.CostEstimate(
            flops=4 * work * HEAD_SIZE, transcendentals=work, bytes_accessed=1
        ),
        name="context_states",
    )(column_slot, *pieces, *keys, *values, *tabs)


def shares_of(ends):
    top = functools.reduce(jnp.maximum, ends)
    shares = [jnp.exp(end - top) for end in ends]
    total = functools.reduce(jnp.add, shares)
    return [share / total for share in shares], top + jnp.log(total)


def mixed(parts, shares, h):
    return functools.reduce(
        jnp.add, [part * share[:, h : h + 1] for part, share in zip(parts, shares)]
    )


def both_halves(i, low_ref, high_ref):
    halves = [r.at[i, h] for r in (low_ref, high_ref) for h in range(r.shape[1] - 1)]
    return halves, low_ref[i, low_ref.shape[1] - 1] + high_ref[i, high_ref.shape[1] - 1]


def home_kernel(
    steps, length_ref, query_ref, tiles, new_key_ref, new_value_ref, low_ref, high_ref, other_ref, *refs
):
    out_ref, wide, key_ref, value_ref = refs[-4:]
    rows, slots = row_count(query_ref), key_ref.shape[0]
    split_rows(tiles, wide, 0, slots, key_ref, value_ref)
    used = lax.broadcasted_iota(jnp.int32, (rows, slots), 1) < length_ref[0]
    step = lax.rem(lax.broadcasted_iota(jnp.int32, (rows, steps), 0), steps)
    seen = lax.broadcasted_iota(jnp.int32, (rows, steps), 1) <= step
    ends, means = jnp.zeros((rows, HEAD_SIZE), jnp.float32), []
    for h in range(KEY_VALUE_HEADS):
        at = head_lanes(h)
        query = rows_of(query_ref.at[0], h)
        cached = lax.dot_general(query, key_ref[:, at], NT, preferred_element_type=jnp.float32)
        fresh = lax.dot_general(query, new_key_ref[:, at], NT, preferred_element_type=jnp.float32)
        cached = jnp.where(used, cached, FILLER)
        fresh = jnp.where(seen, fresh, FILLER)
        mean, end = block_softmax([cached, fresh], [value_ref[:, at], new_value_ref[:, at]])
        means.append(mean)
        ends = put_lane(ends, h, end)
    own, own_end = both_halves(0, low_ref, high_ref)
    shares, end = shares_of([ends, own_end, other_ref[0, KEY_VALUE_HEADS]])
    for h, mean in enumerate(means):
        out_ref[h] = mixed([mean, own[h][...], other_ref[0, h]], shares, h)
    out_ref[KEY_VALUE_HEADS] = end


def home_state(query_message, cache, length, new_keys, new_values, low, high, other, after):
    rows, steps = row_count(query_message), new_keys.shape[0]
    work = rows * KEY_VALUE_HEADS * cache.shape[0]
    tiles = tile_rows(cache)
    return pl.pallas_call(
        functools.partial(home_kernel, steps),
        in_specs=in_smem(1) + in_vmem(7) + in_any(len(after)),
        out_shape=jax.ShapeDtypeStruct((KEY_VALUE_HEADS + 1, rows, HEAD_SIZE), jnp.float32),
        scratch_shapes=[
            pltpu.VMEM(tiles.shape, jnp.float32),
            pltpu.VMEM((cache.shape[0], cache.shape[2]), cache.dtype),
            pltpu.VMEM((cache.shape[0], cache.shape[2]), cache.dtype),
        ],
        compiler_params=pltpu.CompilerParams(vmem_limit_bytes=vmem_limit(low.shape[0])),
        cost_estimate=pl.CostEstimate(
            flops=4 * work * HEAD_SIZE, transcendentals=work, bytes_accessed=4 * cache.size
        ),
        name="home_state",
    )(length, query_message, tiles, new_keys, new_values, low, high, other, *after)


def pair_kernel(order, low_ref, high_ref, other_ref, *coded_refs):
    rows = other_ref.shape[2]
    for (i, at), coded_ref in zip(order, coded_refs):
        own, own_end = both_halves(i, low_ref, high_ref)
        shares, end = shares_of([own_end, other_ref[at, KEY_VALUE_HEADS]])
        means = [
            mixed([own[h][...], other_ref[at, h]], shares, h) for h in range(KEY_VALUE_HEADS)
        ]
        reach = jnp.ones((rows, HEAD_SIZE), jnp.float32)
        for h, mean in enumerate(means):
            reach = put_lane(reach, h, jnp.max(jnp.abs(mean), axis=-1, keepdims=True))
        exponent = jnp.ceil(jnp.log2(jnp.maximum(reach, 1e-30)))
        factor = jnp.exp2(-exponent) * CODE_TOP
        for h, mean in enumerate(means):
            code = jnp.round(mean * factor[:, h : h + 1])
            coded_ref[pl.ds(h * rows, rows)] = code.astype(jnp.int32).astype(jnp.int16)
        near = jnp.round(end)
        rest = jnp.round((end - near) * REST_TOP)
        lane = lax.broadcasted_iota(jnp.int32, (EXTRA, HEAD_SIZE), 1) // KEY_VALUE_HEADS
        slab, kinds = jnp.zeros((EXTRA, HEAD_SIZE), jnp.float32), (near, rest, exponent)
        for r in range(rows // EXTRA):
            for k, kind in enumerate(kinds):
                place = r * len(kinds) + k
                part = kind[r * EXTRA : (r + 1) * EXTRA]
                moved = pltpu.roll(part, place * KEY_VALUE_HEADS, 1) if place else part
                slab = jnp.where(lane == place, moved, slab)
        coded_ref[pl.ds(KEY_VALUE_HEADS * rows, EXTRA)] = slab.astype(jnp.int32).astype(jnp.int16)


def pair_states(order, low, high, other):
    rows = other.shape[2]
    shape = (KEY_VALUE_HEADS * rows + EXTRA, HEAD_SIZE)
    return pl.pallas_call(
        functools.partial(pair_kernel, order),
        out_shape=[jax.ShapeDtypeStruct(shape, jnp.int16)] * len(order),
        compiler_params=pltpu.CompilerParams(vmem_limit_bytes=vmem_limit(low.shape[0])),
        name="pair_states",
    )(low, high, other)


def final_kernel(home_ref, *refs):
    coded_refs, out_ref = refs[:-1], refs[-1]
    rows = home_ref.shape[1]
    ends, factors = [home_ref[KEY_VALUE_HEADS]], []
    head_lane = lax.broadcasted_iota(jnp.int32, ends[0].shape, 1) < KEY_VALUE_HEADS
    for r in coded_refs:
        slab = extra_of(r).astype(jnp.int32).astype(jnp.float32)
        near, rest, exponent = (
            jnp.concatenate(
                [
                    pltpu.roll(slab, (HEAD_SIZE - (3 * i + k) * KEY_VALUE_HEADS) % HEAD_SIZE, 1)
                    for i in range(rows // EXTRA)
                ]
            )
            for k in range(3)
        )
        ends.append(near + rest / REST_TOP)
        factors.append(jnp.exp2(jnp.where(head_lane, exponent, 0.0)) / CODE_TOP)
    shares, _ = shares_of([jnp.where(head_lane, end, 0.0) for end in ends])
    shares = shares[:1] + [share * factor for share, factor in zip(shares[1:], factors)]
    for h in range(KEY_VALUE_HEADS):
        parts = [rows_of(r, h).astype(jnp.int32).astype(jnp.float32) for r in coded_refs]
        out_ref[h] = mixed([home_ref[h]] + parts, shares, h).astype(jnp.bfloat16)


def final_output(home, coded):
    return pl.pallas_call(
        final_kernel,
        out_shape=jax.ShapeDtypeStruct((KEY_VALUE_HEADS,) + home.shape[1:], jnp.bfloat16),
        compiler_params=pltpu.CompilerParams(vmem_limit_bytes=vmem_limit(len(coded))),
        name="final_output",
    )(home, *coded)


def swap(count, bit):
    return [(i, i ^ bit) for i in range(count)]


def shards(
    queries,
    prefix_key_value,
    tab_key_value,
    tab_owner,
    session_tab,
    suffix_key_value,
    suffix_len,
    token_keys,
    token_values,
):
    ctx_count, tab_count = lax.axis_size("ctx"), lax.axis_size("tab")
    pair_count = ctx_count // 2
    steps = queries.shape[1]
    tab_rows = tab_key_value.shape[1]

    query = queries[0].reshape(steps, KEY_VALUE_HEADS, -1, HEAD_SIZE)
    query = query.transpose(1, 2, 0, 3).reshape(-1, HEAD_SIZE)
    message, tab_block = prepare(session_tab, tab_owner, query, tab_key_value[0])
    tabs = [tab_block] + [
        lax.ppermute(tab_block, "tab", swap(tab_count, k)) for k in range(1, tab_count)
    ]
    places = jnp.arange(tab_count * tab_rows, dtype=jnp.int32) // tab_rows
    column_slot = (places ^ lax.axis_index("tab")).astype(jnp.float32)[None]

    tiles = tile_rows(prefix_key_value)
    half = prefix_key_value.shape[0] // 2
    splits = [split_pairs(tiles, i * half, half) for i in range(2)]
    pieces, masks, bit = [message], [0], pair_count // 2
    while bit:
        if len(masks) == 2:
            pieces[-1], splits[0] = lax.optimization_barrier((pieces[-1], splits[0]))
        column = jnp.concatenate(pieces, axis=0) if len(pieces) > 1 else message
        pieces = [column, lax.ppermute(column, "ctx", swap(ctx_count, 2 * bit))]
        masks, bit = masks + [mask ^ bit for mask in masks], bit // 2
    pieces[-1], tabs, splits = lax.optimization_barrier((pieces[-1], tabs, splits))
    other_pieces = [lax.ppermute(piece, "ctx", swap(ctx_count, 1)) for piece in pieces]
    keys, values = zip(*splits)
    shared = (keys, values, column_slot, tabs)
    heads = tuple(range(KEY_VALUE_HEADS))
    first, second = heads[:5], heads[5:]
    members = range(pair_count)
    far = [i for i in members if masks[i] >= pair_count // 2]
    rest = [i for i in members if i not in far]
    (low,) = context_states(first, [members], pieces, *shared)
    other_pieces, low = lax.optimization_barrier((other_pieces, low))
    others = context_states(heads, [far, rest], other_pieces, *shared)
    pieces, others = lax.optimization_barrier((pieces, others))
    others = list(others)
    others[0] = lax.ppermute(others[0], "ctx", swap(ctx_count, 1))
    (high,) = context_states(second, [members], pieces, *shared)
    coded, received = [], []
    for group, other in zip((far, rest), others):
        if coded:
            coded, other = lax.optimization_barrier((coded, other))
            other = others[1] = lax.ppermute(other, "ctx", swap(ctx_count, 1))
        order = [(i, at) for at, i in enumerate(group) if i]
        if order:
            codes = pair_states(order, low, high, other)
            coded += codes
            received += [
                lax.ppermute(code, "ctx", swap(ctx_count, 2 * masks[i]))
                for (i, _), code in zip(order, codes)
            ]
    home = home_state(
        message,
        suffix_key_value[0],
        suffix_len,
        token_keys[0],
        token_values[0],
        low,
        high,
        others[1],
        after=coded,
    )
    result = final_output(home, received)
    result = result.reshape(KEY_VALUE_HEADS, -1, steps, HEAD_SIZE)
    return result.transpose(2, 0, 1, 3).reshape(queries.shape)


def solution(mesh):
    sessions = ("ctx", "tab")
    placed = (
        P(sessions, None, None),
        P("ctx", None, None),
        P("tab", "ctx", None, None),
        P(),
        P(sessions),
        P(sessions, None, None, None),
        P(sessions),
        P(sessions, None, None),
        P(sessions, None, None),
    )
    return jax.shard_map(
        shards, mesh=mesh, in_specs=placed, out_specs=P(sessions, None, None), check_vma=False
    )
```

```python
import functools

import jax
import jax.numpy as jnp
from jax import lax
from jax.experimental import pallas as pl
from jax.experimental.pallas import tpu as pltpu
from jax.sharding import PartitionSpec as P

KEY_VALUE_HEADS = 8
HEAD_SIZE = 128
SCALE = HEAD_SIZE**-0.5
SCALE_TWO = SCALE * 1.4426950408889634
MIB = 1024 * 1024
FILLER = -1e30
CODE_TOP = 32000.0
REST_TOP = 65000.0

NT = (((1,), (1,)), ((), ()))


def head_lanes(h):
    return pl.ds(h * HEAD_SIZE, HEAD_SIZE)


def put_lane(slab, lane, column):
    at = lax.broadcasted_iota(jnp.int32, slab.shape, 1)
    return jnp.where(at == lane, column, slab)


def vmem_limit(members, slots=4):
    return (8 if members * slots <= 32 else 48) * MIB


def in_any(count):
    return [pl.BlockSpec(memory_space=pl.ANY)] * count


def in_hbm(count):
    return [pl.BlockSpec(memory_space=pltpu.HBM)] * count


def in_vmem(count):
    return [pl.BlockSpec(memory_space=pltpu.VMEM)] * count


def in_smem(count):
    return [pl.BlockSpec(memory_space=pltpu.SMEM)] * count


def tile_rows(paired):
    tiles = paired.reshape(paired.shape[0], 2, KEY_VALUE_HEADS, HEAD_SIZE)
    return tiles.transpose(0, 2, 1, 3).reshape(-1, HEAD_SIZE)


PER_ROW = 2 * KEY_VALUE_HEADS
EXTRA = 8


def split_rows(tiles, wide, first, count, key_ref, value_ref):
    start = first * PER_ROW
    wide[pl.ds(start, count * PER_ROW)] = tiles[pl.ds(start, count * PER_ROW)].astype(jnp.float32)
    for h in range(KEY_VALUE_HEADS):
        for k, ref in enumerate((key_ref, value_ref)):
            rows = wide[pl.ds(start + 2 * h + k, count, stride=PER_ROW), :]
            ref[pl.ds(first, count), head_lanes(h)] = rows.astype(ref.dtype)


def prepare_kernel(
    session, owner_hbm, query_hbm, tab_hbm, message_ref, block_ref, tiles, wide, owner, sems
):
    moves = [
        (tab_hbm, tiles),
        (owner_hbm, owner),
        (query_hbm, message_ref.at[0, pl.ds(0, query_hbm.shape[0])]),
    ]
    copies = [pltpu.make_async_copy(*move, sems.at[i]) for i, move in enumerate(moves)]
    for copy in copies:
        copy.start()
    copies[1].wait()
    slot = jnp.int32(0)
    for k in range(owner.shape[0]):
        slot = jnp.where(session[0] == k, owner[k], slot)
    filled = jnp.full((EXTRA, HEAD_SIZE), slot.astype(jnp.float32), jnp.float32)
    message_ref[0, pl.ds(query_hbm.shape[0], EXTRA)] = filled.astype(jnp.bfloat16)
    copies[0].wait()
    split_rows(tiles, wide, 0, block_ref.shape[1], block_ref.at[0], block_ref.at[1])
    copies[2].wait()


def stay(arrays):
    return [pltpu.with_memory_space_constraint(array, pltpu.HBM) for array in arrays]


def prepare(session_tab, tab_owner, query, tab):
    tiles = tile_rows(tab)
    return pl.pallas_call(
        prepare_kernel,
        in_specs=in_smem(1) + in_hbm(3),
        out_specs=in_vmem(2),
        out_shape=[
            jax.ShapeDtypeStruct((1, query.shape[0] + EXTRA, HEAD_SIZE), jnp.bfloat16),
            jax.ShapeDtypeStruct((2, tab.shape[0], tab.shape[2]), jnp.bfloat16),
        ],
        scratch_shapes=[
            pltpu.VMEM(tiles.shape, tiles.dtype),
            pltpu.VMEM(tiles.shape, jnp.float32),
            pltpu.SMEM(tab_owner.shape, tab_owner.dtype),
            pltpu.SemaphoreType.DMA((4,)),
        ],
        compiler_params=pltpu.CompilerParams(vmem_limit_bytes=6 * MIB),
        name="prepare",
    )(session_tab, *stay([tab_owner, query, tiles]))


def split_kernel(first, chunks, tiles_hbm, key_ref, value_ref, tiles, wide, sems):
    rows = key_ref.shape[0] // chunks
    piece = rows * PER_ROW
    copies = [
        pltpu.make_async_copy(
            tiles_hbm.at[pl.ds(first * PER_ROW + i * piece, piece)],
            tiles.at[pl.ds(i * piece, piece)],
            sems.at[i],
        )
        for i in range(chunks)
    ]
    for copy in copies:
        copy.start()
    for i, copy in enumerate(copies):
        copy.wait()
        split_rows(tiles, wide, i * rows, rows, key_ref, value_ref)


def split_pairs(tiles, first, rows, chunks=4):
    shape = jax.ShapeDtypeStruct((rows, KEY_VALUE_HEADS * HEAD_SIZE), tiles.dtype)
    scratch = (rows * PER_ROW, HEAD_SIZE)
    return pl.pallas_call(
        functools.partial(split_kernel, first, chunks),
        in_specs=in_hbm(1),
        out_specs=in_vmem(2),
        out_shape=[shape, shape],
        scratch_shapes=[
            pltpu.VMEM(scratch, tiles.dtype),
            pltpu.VMEM(scratch, jnp.float32),
            pltpu.SemaphoreType.DMA((chunks,)),
        ],
        compiler_params=pltpu.CompilerParams(vmem_limit_bytes=6 * MIB),
        name="split_pairs",
    )(*stay([tiles]))


def block_softmax(score_parts, value_parts):
    largest = functools.reduce(
        jnp.maximum, [jnp.max(s, axis=-1, keepdims=True) for s in score_parts]
    )
    product = 0.0
    for scores, values in zip(score_parts, value_parts):
        weights = jnp.exp2((scores - largest) * SCALE_TWO).astype(jnp.bfloat16)
        values = jnp.concatenate([values, jnp.ones_like(values)], axis=1)
        product += jnp.dot(weights, values, preferred_element_type=jnp.float32)
    summed, total = product[:, :HEAD_SIZE], product[:, HEAD_SIZE:]
    return summed / total, largest * SCALE + jnp.log(total)


def row_count(message):
    return (message.shape[-2] - EXTRA) // KEY_VALUE_HEADS


def rows_of(ref, h):
    rows = row_count(ref)
    return ref[pl.ds(h * rows, rows)]


def extra_of(ref):
    return ref[pl.ds(ref.shape[0] - EXTRA, EXTRA)]


def context_kernel(heads, groups, pieces, shares, slots, column_slot_ref, *refs):
    query_refs = [r.at[i] for r in refs[:pieces] for i in range(r.shape[0])]
    refs = refs[pieces:]
    key_refs, value_refs, refs = refs[:shares], refs[shares : 2 * shares], refs[2 * shares :]
    tab_refs, out_refs, members = refs[:slots], refs[slots:], len(query_refs)
    places = [(i, r.at[n]) for r, group in zip(out_refs, groups) for n, i in enumerate(group)]
    rows = row_count(query_refs[0])
    owner = jnp.concatenate([extra_of(q)[:, 0:1] for q in query_refs for _ in range(rows // EXTRA)])
    mine = owner.astype(jnp.float32) == column_slot_ref[0:1, :]
    ends = jnp.zeros((members * rows, HEAD_SIZE), jnp.float32)
    for n, h in enumerate(heads):
        at = head_lanes(h)
        query = jnp.concatenate([rows_of(q, h) for q in query_refs], axis=0)
        tab_keys = jnp.concatenate([t[0, :, at] for t in tab_refs], axis=0)
        tab_values = jnp.concatenate([t[1, :, at] for t in tab_refs], axis=0)
        scores = [
            lax.dot_general(query, keys, NT, preferred_element_type=jnp.float32)
            for keys in [r[:, at] for r in key_refs] + [tab_keys]
        ]
        scores[-1] = jnp.where(mine, scores[-1], FILLER)
        mean, end = block_softmax(scores, [r[:, at] for r in value_refs] + [tab_values])
        for i, place in places:
            place[n] = mean[i * rows : (i + 1) * rows]
        ends = put_lane(ends, h, end)
    for i, place in places:
        place[len(heads)] = ends[i * rows : (i + 1) * rows]


def context_states(heads, groups, pieces, keys, values, column_slot, tabs):
    members, rows = sum(len(group) for group in groups), row_count(pieces[0])
    key_count = sum(k.shape[0] for k in keys) + column_slot.shape[1]
    work = members * rows * len(heads) * key_count
    return pl.pallas_call(
        functools.partial(context_kernel, heads, groups, len(pieces), len(keys), len(tabs)),
        in_specs=in_vmem(1 + len(pieces) + 2 * len(keys) + len(tabs)),
        out_specs=in_vmem(len(groups)),
        out_shape=[
            jax.ShapeDtypeStruct((len(group), len(heads) + 1, rows, HEAD_SIZE), jnp.float32)
            for group in groups
        ],
        compiler_params=pltpu.CompilerParams(vmem_limit_bytes=vmem_limit(members, len(tabs))),
        cost_estimate=pl.CostEstimate(
            flops=4 * work * HEAD_SIZE, transcendentals=work, bytes_accessed=1
        ),
        name="context_states",
    )(column_slot, *pieces, *keys, *values, *tabs)


def shares_of(ends):
    top = functools.reduce(jnp.maximum, ends)
    shares = [jnp.exp(end - top) for end in ends]
    total = functools.reduce(jnp.add, shares)
    return [share / total for share in shares], top + jnp.log(total)


def mixed(parts, shares, h):
    return functools.reduce(
        jnp.add, [part * share[:, h : h + 1] for part, share in zip(parts, shares)]
    )


def both_halves(i, low_ref, high_ref):
    halves = [r.at[i, h] for r in (low_ref, high_ref) for h in range(r.shape[1] - 1)]
    return halves, low_ref[i, low_ref.shape[1] - 1] + high_ref[i, high_ref.shape[1] - 1]


def home_kernel(
    steps, length_ref, query_ref, tiles, new_key_ref, new_value_ref, low_ref, high_ref, other_ref, *refs
):
    out_ref, wide, key_ref, value_ref = refs[-4:]
    rows, slots = row_count(query_ref), key_ref.shape[0]
    split_rows(tiles, wide, 0, slots, key_ref, value_ref)
    used = lax.broadcasted_iota(jnp.int32, (rows, slots), 1) < length_ref[0]
    step = lax.rem(lax.broadcasted_iota(jnp.int32, (rows, steps), 0), steps)
    seen = lax.broadcasted_iota(jnp.int32, (rows, steps), 1) <= step
    ends, means = jnp.zeros((rows, HEAD_SIZE), jnp.float32), []
    for h in range(KEY_VALUE_HEADS):
        at = head_lanes(h)
        query = rows_of(query_ref.at[0], h)
        cached = lax.dot_general(query, key_ref[:, at], NT, preferred_element_type=jnp.float32)
        fresh = lax.dot_general(query, new_key_ref[:, at], NT, preferred_element_type=jnp.float32)
        cached = jnp.where(used, cached, FILLER)
        fresh = jnp.where(seen, fresh, FILLER)
        mean, end = block_softmax([cached, fresh], [value_ref[:, at], new_value_ref[:, at]])
        means.append(mean)
        ends = put_lane(ends, h, end)
    own, own_end = both_halves(0, low_ref, high_ref)
    shares, end = shares_of([ends, own_end, other_ref[0, KEY_VALUE_HEADS]])
    for h, mean in enumerate(means):
        out_ref[h] = mixed([mean, own[h][...], other_ref[0, h]], shares, h)
    out_ref[KEY_VALUE_HEADS] = end


def home_state(query_message, cache, length, new_keys, new_values, low, high, other, after):
    rows, steps = row_count(query_message), new_keys.shape[0]
    work = rows * KEY_VALUE_HEADS * cache.shape[0]
    tiles = tile_rows(cache)
    return pl.pallas_call(
        functools.partial(home_kernel, steps),
        in_specs=in_smem(1) + in_vmem(7) + in_any(len(after)),
        out_shape=jax.ShapeDtypeStruct((KEY_VALUE_HEADS + 1, rows, HEAD_SIZE), jnp.float32),
        scratch_shapes=[
            pltpu.VMEM(tiles.shape, jnp.float32),
            pltpu.VMEM((cache.shape[0], cache.shape[2]), cache.dtype),
            pltpu.VMEM((cache.shape[0], cache.shape[2]), cache.dtype),
        ],
        compiler_params=pltpu.CompilerParams(vmem_limit_bytes=vmem_limit(low.shape[0])),
        cost_estimate=pl.CostEstimate(
            flops=4 * work * HEAD_SIZE, transcendentals=work, bytes_accessed=4 * cache.size
        ),
        name="home_state",
    )(length, query_message, tiles, new_keys, new_values, low, high, other, *after)


def pair_kernel(order, low_ref, high_ref, other_ref, *coded_refs):
    rows = other_ref.shape[2]
    for (i, at), coded_ref in zip(order, coded_refs):
        own, own_end = both_halves(i, low_ref, high_ref)
        shares, end = shares_of([own_end, other_ref[at, KEY_VALUE_HEADS]])
        means = [
            mixed([own[h][...], other_ref[at, h]], shares, h) for h in range(KEY_VALUE_HEADS)
        ]
        reach = jnp.ones((rows, HEAD_SIZE), jnp.float32)
        for h, mean in enumerate(means):
            reach = put_lane(reach, h, jnp.max(jnp.abs(mean), axis=-1, keepdims=True))
        exponent = jnp.ceil(jnp.log2(jnp.maximum(reach, 1e-30)))
        factor = jnp.exp2(-exponent) * CODE_TOP
        for h, mean in enumerate(means):
            code = jnp.round(mean * factor[:, h : h + 1])
            coded_ref[pl.ds(h * rows, rows)] = code.astype(jnp.int32).astype(jnp.int16)
        near = jnp.round(end)
        rest = jnp.round((end - near) * REST_TOP)
        lane = lax.broadcasted_iota(jnp.int32, (EXTRA, HEAD_SIZE), 1) // KEY_VALUE_HEADS
        slab, kinds = jnp.zeros((EXTRA, HEAD_SIZE), jnp.float32), (near, rest, exponent)
        for r in range(rows // EXTRA):
            for k, kind in enumerate(kinds):
                place = r * len(kinds) + k
                part = kind[r * EXTRA : (r + 1) * EXTRA]
                moved = pltpu.roll(part, place * KEY_VALUE_HEADS, 1) if place else part
                slab = jnp.where(lane == place, moved, slab)
        coded_ref[pl.ds(KEY_VALUE_HEADS * rows, EXTRA)] = slab.astype(jnp.int32).astype(jnp.int16)


def pair_states(order, low, high, other):
    rows = other.shape[2]
    shape = (KEY_VALUE_HEADS * rows + EXTRA, HEAD_SIZE)
    return pl.pallas_call(
        functools.partial(pair_kernel, order),
        out_shape=[jax.ShapeDtypeStruct(shape, jnp.int16)] * len(order),
        compiler_params=pltpu.CompilerParams(vmem_limit_bytes=vmem_limit(low.shape[0])),
        name="pair_states",
    )(low, high, other)


def final_kernel(home_ref, *refs):
    coded_refs, out_ref = refs[:-1], refs[-1]
    rows = home_ref.shape[1]
    ends, factors = [home_ref[KEY_VALUE_HEADS]], []
    head_lane = lax.broadcasted_iota(jnp.int32, ends[0].shape, 1) < KEY_VALUE_HEADS
    for r in coded_refs:
        slab = extra_of(r).astype(jnp.int32).astype(jnp.float32)
        near, rest, exponent = (
            jnp.concatenate(
                [
                    pltpu.roll(slab, (HEAD_SIZE - (3 * i + k) * KEY_VALUE_HEADS) % HEAD_SIZE, 1)
                    for i in range(rows // EXTRA)
                ]
            )
            for k in range(3)
        )
        ends.append(near + rest / REST_TOP)
        factors.append(jnp.exp2(jnp.where(head_lane, exponent, 0.0)) / CODE_TOP)
    shares, _ = shares_of([jnp.where(head_lane, end, 0.0) for end in ends])
    shares = shares[:1] + [share * factor for share, factor in zip(shares[1:], factors)]
    for h in range(KEY_VALUE_HEADS):
        parts = [rows_of(r, h).astype(jnp.int32).astype(jnp.float32) for r in coded_refs]
        out_ref[h] = mixed([home_ref[h]] + parts, shares, h).astype(jnp.bfloat16)


def final_output(home, coded):
    return pl.pallas_call(
        final_kernel,
        out_shape=jax.ShapeDtypeStruct((KEY_VALUE_HEADS,) + home.shape[1:], jnp.bfloat16),
        compiler_params=pltpu.CompilerParams(vmem_limit_bytes=vmem_limit(len(coded))),
        name="final_output",
    )(home, *coded)


def swap(count, bit):
    return [(i, i ^ bit) for i in range(count)]


def shards(
    queries,
    prefix_key_value,
    tab_key_value,
    tab_owner,
    session_tab,
    suffix_key_value,
    suffix_len,
    token_keys,
    token_values,
):
    ctx_count, tab_count = lax.axis_size("ctx"), lax.axis_size("tab")
    pair_count = ctx_count // 2
    steps = queries.shape[1]
    tab_rows = tab_key_value.shape[1]

    query = queries[0].reshape(steps, KEY_VALUE_HEADS, -1, HEAD_SIZE)
    query = query.transpose(1, 2, 0, 3).reshape(-1, HEAD_SIZE)
    message, tab_block = prepare(session_tab, tab_owner, query, tab_key_value[0])
    tabs = [tab_block] + [
        lax.ppermute(tab_block, "tab", swap(tab_count, k)) for k in range(1, tab_count)
    ]
    places = jnp.arange(tab_count * tab_rows, dtype=jnp.int32) // tab_rows
    column_slot = (places ^ lax.axis_index("tab")).astype(jnp.float32)[None]

    tiles = tile_rows(prefix_key_value)
    half = prefix_key_value.shape[0] // 2
    splits = [split_pairs(tiles, i * half, half) for i in range(2)]
    pieces, masks, bit = [message], [0], pair_count // 2
    while bit:
        if len(masks) == 2:
            pieces[-1], splits[0] = lax.optimization_barrier((pieces[-1], splits[0]))
        column = jnp.concatenate(pieces, axis=0) if len(pieces) > 1 else message
        pieces = [column, lax.ppermute(column, "ctx", swap(ctx_count, 2 * bit))]
        masks, bit = masks + [mask ^ bit for mask in masks], bit // 2
    pieces[-1], tabs, splits = lax.optimization_barrier((pieces[-1], tabs, splits))
    other_pieces = [lax.ppermute(piece, "ctx", swap(ctx_count, 1)) for piece in pieces]
    keys, values = zip(*splits)
    shared = (keys, values, column_slot, tabs)
    heads = tuple(range(KEY_VALUE_HEADS))
    first, second = heads[:5], heads[5:]
    members = range(pair_count)
    far = [i for i in reversed(members) if masks[i] >= pair_count // 2]
    rest = [i for i in members if i not in far]
    (low,) = context_states(first, [members], pieces, *shared)
    other_pieces, low = lax.optimization_barrier((other_pieces, low))
    others = context_states(heads, [far, rest], other_pieces, *shared)
    pieces, others = lax.optimization_barrier((pieces, others))
    others = list(others)
    others[0] = lax.ppermute(others[0], "ctx", swap(ctx_count, 1))
    (high,) = context_states(second, [members], pieces, *shared)
    coded, received = [], []
    for group, other in zip((far, rest), others):
        if coded:
            coded, other = lax.optimization_barrier((coded, other))
            other = others[1] = lax.ppermute(other, "ctx", swap(ctx_count, 1))
        order = [(i, at) for at, i in enumerate(group) if i]
        if order:
            codes = pair_states(order, low, high, other)
            coded += codes
            received += [
                lax.ppermute(code, "ctx", swap(ctx_count, 2 * masks[i]))
                for (i, _), code in zip(order, codes)
            ]
    home = home_state(
        message,
        suffix_key_value[0],
        suffix_len,
        token_keys[0],
        token_values[0],
        low,
        high,
        others[1],
        after=coded,
    )
    result = final_output(home, received)
    result = result.reshape(KEY_VALUE_HEADS, -1, steps, HEAD_SIZE)
    return result.transpose(2, 0, 1, 3).reshape(queries.shape)


def solution(mesh):
    sessions = ("ctx", "tab")
    placed = (
        P(sessions, None, None),
        P("ctx", None, None),
        P("tab", "ctx", None, None),
        P(),
        P(sessions),
        P(sessions, None, None, None),
        P(sessions),
        P(sessions, None, None),
        P(sessions, None, None),
    )
    return jax.shard_map(
        shards, mesh=mesh, in_specs=placed, out_specs=P(sessions, None, None), check_vma=False
    )
```
